32 devices in a mesh: mode: 16 (over z, y, x), real: 2 (over core).
Axes of the slice: x: 2, y: 2, z: 4, core: 2. Of those that a mesh axis runs over, the one named last changes fastest.
Arguments:
- input_field: bfloat16 [2, 2, 256, 16384], P(None, 'real', 'mode'), may hold values from -6 to 6
- kerr_coeff: bfloat16 [16, 64, 64], P('mode'), may hold values from -0.375 to 0.375
- block_list: int32 [16, 4], P('mode'), may hold values from 0 to 31
Outputs:
- density: float32 [512, 2, 256, 256], P('mode', None, 'real')
The draws below stay inside these ranges and needn't reach their ends.
All inputs are finite; a program needn't handle non-finite values.
Results may differ from the reference program's by a relative error of at most 0.0085.
Values may be sent and summed in bfloat16 or wider, within the bound.
A program may use at most 64 MiB of HBM per device.

```python
import jax
import jax.numpy as jnp
from jax import lax

P_SIZE = 256
MB = 8
FT = 128
NB = 512
R_DEV = 1
NT = 16384
NMB = 32
FB = 32
NBLK = 16
RE = 2
N_REAL = 2


def with_ends(values, rng, smallest, top_value):
    longest = values.shape.index(max(values.shape))
    spots = []
    for shift in (0, 1):
        where = [jax.random.randint(jax.random.fold_in(rng, axis), (), 0, length) for axis, length in enumerate(values.shape)]
        where[longest] = (where[longest] + shift) % values.shape[longest]
        spots.append(tuple(where))
    return values.at[spots[0]].set(smallest).at[spots[1]].set(top_value)


def levels(stream_key, dims, split, least, largest):
    factor_of = 1.0
    for axis_at, parts in split:
        steps = jax.random.uniform(jax.random.fold_in(jax.random.fold_in(stream_key, 6), axis_at), (parts,), jnp.float32, least / len(split), largest / len(split))
        factor_of = factor_of * jnp.repeat(jnp.exp(steps), dims[axis_at] // parts).reshape((-1,) + (1,) * (len(dims) - 1 - axis_at))
    return factor_of


def normal_values(stream_key, shape, spread, limit, pieces=(), kind=jnp.bfloat16):
    drawn = spread * jax.random.normal(stream_key, shape, jnp.float32)
    if pieces:
        drawn = drawn * levels(stream_key, shape, pieces, -0.22, 0.18)
    return jnp.clip(drawn, -limit, limit).astype(kind)


def setup_inputs(seed: int = 0) -> dict:
    arg_keys = jax.random.split(jax.random.key(seed), 4)
    input_field = normal_values(arg_keys[0], (2, RE, P_SIZE, NT), 1.0, 6.0, ((1, 2), (2, 16)))
    kerr_coeff = normal_values(arg_keys[1], (NBLK, MB * MB, MB * MB), (16 * NBLK) ** -0.5, 0.375, ((0, 16),))
    block_list = with_ends(jax.random.randint(arg_keys[2], (NBLK, 4), 0, NMB), jax.random.fold_in(arg_keys[2], 1), 0, NMB - 1).astype(jnp.int32)
    return dict(input_field=input_field, kerr_coeff=kerr_coeff, block_list=block_list)


kerr_strength = 0.25


def band_product(rows_part, cols_part):
    return jnp.einsum("rpbf,rqbf->bpq", rows_part.astype(jnp.float32), cols_part.astype(jnp.float32), precision=lax.Precision.HIGHEST)


def reference(input_field, kerr_coeff, block_list):
    total_real = R_DEV * N_REAL
    field_blocks = input_field.reshape(2, total_real, NMB, MB, NT)

    def add_block(running, item):
        coeff_one, block_one = item
        mode_l = lax.dynamic_index_in_dim(field_blocks, block_one[1], 2, keepdims=False).astype(jnp.float32)
        mode_m = lax.dynamic_index_in_dim(field_blocks, block_one[2], 2, keepdims=False).astype(jnp.float32)
        mode_n = lax.dynamic_index_in_dim(field_blocks, block_one[3], 2, keepdims=False).astype(jnp.float32)
        prod_re = mode_m[0][:, :, None, :] * mode_n[0][:, None, :, :] + mode_m[1][:, :, None, :] * mode_n[1][:, None, :, :]
        prod_im = mode_m[1][:, :, None, :] * mode_n[0][:, None, :, :] - mode_m[0][:, :, None, :] * mode_n[1][:, None, :, :]
        pairs = jnp.stack([prod_re, prod_im]).reshape(2, total_real, MB * MB, NT).astype(jnp.bfloat16)
        weighted = jnp.einsum("ab,crbt->crat", coeff_one.astype(jnp.float32), pairs.astype(jnp.float32), precision=lax.Precision.HIGHEST)
        weighted = weighted.reshape(2, total_real, MB, MB, NT)
        term_re = jnp.sum(weighted[0] * mode_l[0][:, None] - weighted[1] * mode_l[1][:, None], axis=2)
        term_im = jnp.sum(weighted[0] * mode_l[1][:, None] + weighted[1] * mode_l[0][:, None], axis=2)
        target = block_one[0]
        before = lax.dynamic_index_in_dim(running, target, 2, keepdims=False)
        running = lax.dynamic_update_index_in_dim(running, before + jnp.stack([term_re, term_im]), target, 2)
        return running, None

    initial = jnp.zeros((2, total_real, NMB, MB, NT), jnp.float32)
    kerr_sum, unused = lax.scan(add_block, initial, (kerr_coeff, block_list))
    kerr_sum = kerr_sum.reshape(2, total_real, P_SIZE, NT)
    base = input_field.astype(jnp.float32)
    stepped_re = (base[0] - kerr_strength * kerr_sum[1]).astype(jnp.bfloat16)
    stepped_im = (base[1] + kerr_strength * kerr_sum[0]).astype(jnp.bfloat16)
    spectrum = jnp.fft.fft(lax.complex(stepped_re.astype(jnp.float32), stepped_im.astype(jnp.float32)), axis=-1) / FT
    spec_re = lax.optimization_barrier(jnp.real(spectrum).astype(jnp.bfloat16))
    spec_im = lax.optimization_barrier(jnp.imag(spectrum).astype(jnp.bfloat16))
    band_re = spec_re.reshape(total_real, P_SIZE, NB, FB)
    band_im = spec_im.reshape(total_real, P_SIZE, NB, FB)
    dens_re = band_product(band_re, band_re) + band_product(band_im, band_im)
    dens_im = band_product(band_im, band_re) - band_product(band_re, band_im)
    return jnp.stack([dens_re, dens_im], axis=1) / (FB * total_real)
```

```python
import functools
import math

import jax
import jax.numpy as jnp
import numpy as np
from jax import lax
from jax.experimental import pallas as pl
from jax.experimental.pallas import tpu as pltpu
from jax.sharding import PartitionSpec as P

MB = 8
FT = 128
NT = 16384
FB = 32


kerr_strength = 0.25


def kerr_terms(field_blocks, coeff_group, block_group):
    mode_l = jnp.take(field_blocks, block_group[:, 1], axis=2).astype(jnp.float32)
    mode_m = jnp.take(field_blocks, block_group[:, 2], axis=2).astype(jnp.float32)
    mode_n = jnp.take(field_blocks, block_group[:, 3], axis=2).astype(jnp.float32)
    realiz = field_blocks.shape[1]
    group_size = block_group.shape[0]
    steps_local = field_blocks.shape[4]
    prod_re = (
        mode_m[0][:, :, :, None, :] * mode_n[0][:, :, None, :, :]
        + mode_m[1][:, :, :, None, :] * mode_n[1][:, :, None, :, :]
    )
    prod_im = (
        mode_m[1][:, :, :, None, :] * mode_n[0][:, :, None, :, :]
        - mode_m[0][:, :, :, None, :] * mode_n[1][:, :, None, :, :]
    )
    pairs = (
        jnp.stack([prod_re, prod_im])
        .reshape(2, realiz, group_size, MB * MB, steps_local)
        .astype(jnp.bfloat16)
    )
    weighted = jnp.einsum(
        "kab,crkbt->crkat", coeff_group, pairs, preferred_element_type=jnp.float32
    )
    weighted = weighted.reshape(2, realiz, group_size, MB, MB, steps_local)
    term_re = jnp.sum(
        weighted[0] * mode_l[0][:, :, None] - weighted[1] * mode_l[1][:, :, None], axis=3
    )
    term_im = jnp.sum(
        weighted[0] * mode_l[1][:, :, None] + weighted[1] * mode_l[0][:, :, None], axis=3
    )
    one_hot = (
        block_group[:, 0][:, None] == jnp.arange(field_blocks.shape[2], dtype=jnp.int32)[None, :]
    ).astype(jnp.float32)
    return jnp.einsum(
        "kg,crkpt->crgpt", one_hot, jnp.stack([term_re, term_im]), precision=lax.Precision.HIGHEST
    )


def phase_table(extent, modulus):
    index_a = jnp.arange(extent, dtype=jnp.int32)[:, None]
    index_b = jnp.arange(extent, dtype=jnp.int32)[None, :]
    angle = 2.0 * math.pi / modulus * (index_a * index_b % modulus).astype(jnp.float32)
    return (jnp.cos(angle), -jnp.sin(angle))


def first_pass(table, data):
    table_high = table.astype(jnp.bfloat16)
    table_low = (table - table_high.astype(jnp.float32)).astype(jnp.bfloat16)
    upper = jnp.einsum("kn,rmnj->rmkj", table_high, data, preferred_element_type=jnp.float32)
    return upper + jnp.einsum("kn,rmnj->rmkj", table_low, data, preferred_element_type=jnp.float32)


def second_pass(table, data):
    return jnp.einsum("jn,rmkn->rmjk", table, data, precision=lax.Precision.HIGH)


def transform(by_mode):
    realiz = by_mode.shape[1]
    local_modes = by_mode.shape[2]
    signal = by_mode.reshape(2, realiz, local_modes, FT, FT)
    four_re, four_im = phase_table(FT, FT)
    twist_re, twist_im = phase_table(FT, NT)
    half_re = first_pass(four_re, signal[0]) - first_pass(four_im, signal[1])
    half_im = first_pass(four_re, signal[1]) + first_pass(four_im, signal[0])
    turned_re = half_re * twist_re - half_im * twist_im
    turned_im = half_re * twist_im + half_im * twist_re
    out_re = (second_pass(four_re, turned_re) - second_pass(four_im, turned_im)) / FT
    out_im = (second_pass(four_re, turned_im) + second_pass(four_im, turned_re)) / FT
    return jnp.stack([out_re, out_im]).astype(jnp.bfloat16)


def gram_parts(rows_part, cols_part):
    mode_parts = jnp.einsum(
        "crpbf,drqbf->bcdpq", rows_part, cols_part, preferred_element_type=jnp.float32
    )
    return jnp.stack(
        [mode_parts[:, 0, 0] + mode_parts[:, 1, 1], mode_parts[:, 1, 0] - mode_parts[:, 0, 1]], axis=1
    )


def shards(input_field, kerr_coeff, block_list):
    timed = lax.all_to_all(input_field, "mode", split_axis=3, concat_axis=2, tiled=True)
    realiz = timed.shape[1]
    width = timed.shape[2]
    steps_local = timed.shape[3]
    field_blocks = timed.reshape(2, realiz, width // MB, MB, steps_local)
    initial = jnp.zeros(field_blocks.shape, jnp.float32)
    running = initial
    coeff_piece = lax.all_gather(kerr_coeff, "mode", axis=0, tiled=True)
    block_piece = lax.all_gather(block_list, "mode", axis=0, tiled=True)
    block_count = block_piece.shape[0]
    coeff_groups = coeff_piece.reshape(
        block_count // 8, 8, coeff_piece.shape[1], coeff_piece.shape[2]
    )
    block_groups = block_piece.reshape(block_count // 8, 8, 4)

    def one_group(carried, groups):
        return (carried + kerr_terms(field_blocks, groups[0], groups[1]), None)

    running, unused = lax.scan(one_group, running, (coeff_groups, block_groups))
    kerr_sum = running
    kerr_sum = kerr_sum.reshape(2, realiz, width, steps_local)
    base = timed.astype(jnp.float32)
    stepped = jnp.stack(
        [base[0] - kerr_strength * kerr_sum[1], base[1] + kerr_strength * kerr_sum[0]]
    ).astype(jnp.bfloat16)
    by_mode = lax.all_to_all(stepped, "mode", split_axis=2, concat_axis=3, tiled=True)
    spectrum = transform(by_mode)
    banded = lax.all_to_all(spectrum, "mode", split_axis=3, concat_axis=2, tiled=True)
    bands_dev = banded.shape[3] * FT // FB
    spec_bands = banded.reshape(2, realiz, width, bands_dev, FB)
    scale = 1.0 / (FB * realiz * lax.axis_size("real"))
    row_count = width // lax.axis_size("real")
    row_first = lax.axis_index("real") * row_count
    shard_piece = lax.all_gather(spec_bands, "real", axis=1, tiled=True)
    own_part = lax.dynamic_slice_in_dim(shard_piece, row_first, row_count, 2)
    return gram_parts(own_part, shard_piece) * scale


VMEM = pltpu.VMEM
ANY = pl.ANY
HALF = jnp.bfloat16
SUB = 8


def plane_size(parts):
    return 4 if parts % 4 == 0 else 1


def partner_order(parts):
    plane = plane_size(parts)
    return sorted(range(1, parts), key=lambda step: (-(step // plane), step))


def partner(me, step):
    to, bit = me, 1
    while bit <= step:
        if step & bit:
            to = to + bit - 2 * bit * (me // bit % 2)
        bit *= 2
    return to


def remote(here, there, sent, landed, target):
    copy = pltpu.make_async_remote_copy(
        src_ref=here,
        dst_ref=there,
        send_sem=sent,
        recv_sem=landed,
        device_id=target,
        device_id_type=pl.DeviceIdType.MESH,
    )
    copy.start()
    return copy


def local(here, there, sem):
    copy = pltpu.make_async_copy(here, there, sem)
    copy.start()
    return copy


def kerr_terms_of(k, list_s, coef, fld, terms):
    piece = fld.shape[3]
    bl, bm, bn = (list_s[k, 0, i] for i in (1, 2, 3))
    m_re, m_im = fld[0, bm][:, None], fld[1, bm][:, None]
    n_re, n_im = fld[0, bn][None], fld[1, bn][None]
    p_re = (m_re * n_re + m_im * n_im).reshape(MB * MB, piece)
    p_im = (m_im * n_re - m_re * n_im).reshape(MB * MB, piece)
    pairs = jnp.concatenate([p_re, p_im], axis=1).astype(HALF)
    w = jnp.dot(coef, pairs, preferred_element_type=jnp.float32)
    w_re = w[:, :piece].reshape(MB, MB, piece)
    w_im = w[:, piece:].reshape(MB, MB, piece)
    l_re, l_im = fld[0, bl][:, None], fld[1, bl][:, None]
    at = pl.ds(pl.multiple_of(k * MB, MB), MB)
    terms[0, at] = jnp.sum(w_re * l_re - w_im * l_im, axis=0)
    terms[1, at] = jnp.sum(w_re * l_im + w_im * l_re, axis=0)


def owner_table(blocks, width, list_s):
    shape = (width, blocks * MB)
    row = lax.broadcasted_iota(jnp.int32, shape, 0)
    col = lax.broadcasted_iota(jnp.int32, shape, 1)
    wanted = jnp.full(shape, -1, jnp.int32)
    for k in range(blocks):
        wanted = jnp.where(col // MB == k, list_s[k, 0, 0] * MB + col % MB, wanted)
    return (row == wanted).astype(jnp.float32).astype(HALF)


def swap_rows(coef):
    order_of = (MB * MB, MB * MB)
    row = lax.broadcasted_iota(jnp.int32, order_of, 0)
    col = lax.broadcasted_iota(jnp.int32, order_of, 1)
    swap = (col == (row % MB) * MB + row // MB).astype(jnp.float32).astype(HALF)
    return jnp.dot(swap, coef, preferred_element_type=jnp.float32).astype(HALF)


def pack_coef(coef):
    rows = coef.shape[0] // 2
    return jnp.concatenate([coef[:rows], coef[rows:]], axis=1)


def unpack_coef(packed):
    lanes = packed.shape[1] // 2
    return jnp.concatenate([packed[:, :lanes], packed[:, lanes:]], axis=0)


def whole_kernel(parts, sides, pieces, x_ref, coef_ref, list_ref, *refs):
    table_refs, out_ref = refs[:6], refs[6]
    (timed, coef_in, coef_own, coefs, lists, list_s, fld, terms, stepped, by_mode, xf, rows, spec) = refs[7:20]
    tables, (sends, recvs, own_sems) = refs[20:26], refs[26:]
    me = lax.axis_index("mode")
    other = {"real": 1 - lax.axis_index("real")}
    _, modes, times = x_ref.shape
    steps = times // parts
    width = parts * modes
    groups = width // MB
    half = steps // pieces
    tiles = half // FT
    fine = steps // FT
    halves = modes // SUB
    order = partner_order(parts)
    plane = plane_size(parts)
    barrier = pltpu.get_barrier_semaphore()
    for step in order:
        to = {"mode": partner(me, step)}
        pl.semaphore_signal(barrier, inc=1, device_id=to, device_id_type=pl.DeviceIdType.MESH)
    if sides > 1:
        pl.semaphore_signal(barrier, inc=1, device_id=other, device_id_type=pl.DeviceIdType.MESH)

    local(coef_ref, coef_in, own_sems.at[0]).wait()
    early = [local(a, b, own_sems.at[4 + i]) for i, (a, b) in enumerate(zip(table_refs, tables))]
    coef_own[...] = pack_coef(swap_rows(coef_in[...]))
    pl.semaphore_wait(barrier, parts - 1 + (sides > 1))

    slot = iter(range(sends.shape[0]))
    column, row_of = me % plane, me // plane

    def send_all(here, there, steps_of=order):
        at = next(slot)
        return [
            remote(here(partner(me, step)), there, sends.at[at, step], recvs.at[at, step],
                   {"mode": partner(me, step)})
            for step in steps_of
        ]

    own_coef = coefs.at[column, row_of]
    first = send_all(lambda to: coef_own, own_coef, [step for step in order if step % plane == 0])
    first.append(local(coef_own, own_coef, own_sems.at[0]))
    listed = send_all(lambda to: list_ref, lists.at[me])
    listed.append(local(list_ref, lists.at[me], own_sems.at[1]))

    def chunk(to, part):
        at = pl.multiple_of(to * steps + part * half, FT)
        return x_ref.at[:, :, pl.ds(at, half)]

    def send_field(part):
        copies = send_all(lambda to: chunk(to, part), timed.at[part, me])
        copies.append(local(chunk(me, part), timed.at[part, me], own_sems.at[10 + part]))
        return copies

    field_copies = [send_field(0)]
    for copy in first:
        copy.wait()
    second = send_all(lambda to: coefs.at[column], coefs.at[column],
                      [step for step in order if step < plane])
    field_copies += [send_field(part) for part in range(1, pieces)]
    for copy in listed:
        copy.wait()
    local(lists, list_s, own_sems.at[2]).wait()
    blocks = lists.shape[0]
    owners = owner_table(blocks, width, list_s)
    for copy in second:
        copy.wait()

    mode_copies = [[] for _ in range(halves)]
    mode_slot = {}

    def send_stepped(part, h):
        copies = send_all(lambda to: stepped.at[part, h, to], by_mode.at[part, h, me])
        copies.append(
            local(stepped.at[part, h, me], by_mode.at[part, h, me], own_sems.at[20 + part * halves + h])
        )
        mode_copies[h].append((part, copies))

    early_parts = max(pieces - 2, 0)
    for part, copies in enumerate(field_copies):
        for copy in copies:
            copy.wait()
        for c in range(2):
            fld[c] = timed[part, :, c].astype(jnp.float32).reshape(groups, MB, half)

        def one_block(k, carry):
            kerr_terms_of(k, list_s, unpack_coef(coefs[k % plane, k // plane]), fld, terms)
            return carry

        lax.fori_loop(0, blocks, one_block, 0, unroll=2)
        for c in range(2):
            term = terms[1 - c]
            high = term.astype(HALF)
            low = (term - high.astype(jnp.float32)).astype(HALF)
            kerr = jnp.dot(owners, high, preferred_element_type=jnp.float32)
            kerr = kerr + jnp.dot(owners, low, preferred_element_type=jnp.float32)
            turn = kerr_strength * (2 * c - 1)
            new = fld[c].reshape(width, half) + turn * kerr
            new = new.reshape(parts, halves, SUB, half)
            for h in range(halves):
                stack = [new[:, h, :, n * FT : (n + 1) * FT] for n in range(tiles)]
                stepped[part, h, :, c] = jnp.concatenate(stack, axis=1).astype(HALF)
        if part < early_parts:
            for h in range(halves):
                send_stepped(part, h)
    for h in range(halves):
        for part in range(early_parts, pieces):
            send_stepped(part, h)
    for copy in early:
        copy.wait()

    def send_spectra(h):
        copies = send_all(lambda to: spec.at[h, to], out_ref.at[0, h, me])
        own = local(spec.at[h, me], out_ref.at[0, h, me], own_sems.at[3 if h else 0])
        passed = []
        if sides > 1:
            at = next(slot)
            passed.append(remote(spec.at[h, me], out_ref.at[1, h, me], sends.at[at, 0], recvs.at[at, 0], other))
        else:
            at = None
        return copies, own, passed, at

    outgoing = []
    for h in range(halves):
        for part, copies in mode_copies[h]:
            for copy in copies:
                copy.wait()
            for c in range(2):
                for n in range(tiles):
                    xf[c, :, part * tiles + n] = by_mode[
                        part, h, :, c, n * SUB : (n + 1) * SUB
                    ].astype(jnp.float32)
        dft_modes(xf, rows, tables)
        spec[h] = rows[...].reshape(spec.shape[1:]).astype(HALF)
        outgoing.append(send_spectra(h))
    for h, (copies, own, passed, at) in enumerate(outgoing):
        for step, copy in zip(order, copies):
            copy.wait_recv()
            if sides > 1:
                source = partner(me, step)
                passed.append(
                    remote(out_ref.at[0, h, source], out_ref.at[1, h, source],
                           sends.at[at, step], recvs.at[at, step], other)
                )
    for copies, own, passed, _ in outgoing:
        own.wait()
        for copy in copies:
            copy.wait_send()
        for copy in passed:
            copy.wait()


def spectra_of(field, coef, listed, parts, sides):
    _, modes, times = field.shape
    steps = times // parts
    width = parts * modes
    fine = steps // FT
    halves = modes // SUB
    pieces = max(fine // 2, 1)
    half = steps // pieces
    tiles = half // FT
    plane = plane_size(parts)
    tables = dft_tables()
    slots = 3 + pieces * (1 + halves) + 2 * halves
    packed = (coef.shape[0] // 2, coef.shape[1] * 2)
    spread = (halves, parts, fine, 2 * SUB, FT)
    return pl.pallas_call(
        functools.partial(whole_kernel, parts, sides, pieces),
        out_shape=jax.ShapeDtypeStruct((sides,) + spread, HALF),
        in_specs=[pl.BlockSpec(memory_space=pltpu.HBM)] * (3 + len(tables)),
        out_specs=pl.BlockSpec(memory_space=ANY),
        scratch_shapes=[
            VMEM((pieces, parts, 2, modes, half), HALF),
            VMEM(coef.shape, HALF),
            VMEM(packed, HALF),
            VMEM((plane, parts // plane) + packed, HALF),
            VMEM((parts,) + listed.shape, jnp.int32),
            pltpu.SMEM((parts,) + listed.shape, jnp.int32),
            VMEM((2, width // MB, MB, half), jnp.float32),
            VMEM((2, parts * MB, half), jnp.float32),
            VMEM((pieces, halves, parts, 2, tiles * SUB, FT), HALF),
            VMEM((pieces, halves, parts, 2, tiles * SUB, FT), HALF),
            VMEM((2, parts, fine, SUB, FT), jnp.float32),
            VMEM((2 * FT * SUB, FT), jnp.float32),
            VMEM(spread, HALF),
        ]
        + [VMEM(t.shape, t.dtype) for t in tables]
        + [
            pltpu.SemaphoreType.DMA((slots, parts)),
            pltpu.SemaphoreType.DMA((slots, parts)),
            pltpu.SemaphoreType.DMA((20 + pieces * halves,)),
        ],
        compiler_params=pltpu.CompilerParams(
            collective_id=0, has_side_effects=True, vmem_limit_bytes=28 * 1024 * 1024
        ),
    )(*(pltpu.with_memory_space_constraint(a, pltpu.HBM) for a in (field, coef, listed, *tables)))


def dft_tables():
    a = np.arange(FT)
    four = np.exp(-2j * np.pi / FT * (np.outer(a, a) % FT))
    twist = np.exp(-2j * np.pi / NT * (np.outer(a, a) % NT)) / FT
    first = np.block([[four.real, -four.imag], [four.imag, four.real]])
    second = first.reshape(2, FT, 2 * FT).transpose(1, 0, 2).reshape(2 * FT, 2 * FT)

    def split(t):
        t = t.astype(np.float32)
        high = t.astype(HALF)
        return high, (t - high.astype(np.float32)).astype(HALF)

    return (
        *split(first),
        twist.real.astype(np.float32),
        twist.imag.astype(np.float32),
        *split(second),
    )


def dft_modes(xf, rows, tables):
    f1h, f1l, tw_re, tw_im, f2h, f2l = tables
    flat = xf.reshape(2 * FT * SUB, FT)
    nt = (((1,), (1,)), ((), ()))
    dot = functools.partial(jnp.dot, preferred_element_type=jnp.float32)
    dot_nt = functools.partial(
        lax.dot_general, dimension_numbers=nt, preferred_element_type=jnp.float32
    )
    for m in range(0, SUB, 2):
        x = jnp.concatenate(
            [flat[pl.ds(m + i, 2 * FT, stride=SUB), :].astype(HALF) for i in range(2)], axis=1
        )
        half = dot(f1h[...], x) + dot(f1l[...], x)
        turned = []
        for i in range(2):
            h_re, h_im = half[:FT, i * FT : (i + 1) * FT], half[FT:, i * FT : (i + 1) * FT]
            turned.append(
                jnp.concatenate(
                    [
                        h_re * tw_re[...] - h_im * tw_im[...],
                        h_re * tw_im[...] + h_im * tw_re[...],
                    ],
                    axis=1,
                )
            )
        turned = jnp.concatenate(turned, axis=0)
        high = turned.astype(HALF)
        low = (turned - high.astype(jnp.float32)).astype(HALF)
        out = dot_nt(f2h[...], high) + dot_nt(f2h[...], low) + dot_nt(f2l[...], high)
        for i in range(2):
            rows[pl.ds(m + i, 2 * FT, stride=SUB), :] = out[:, i * FT : (i + 1) * FT]


def gram_kernel(scale, spec_ref, out_ref, held, sems):
    sides, halves, parts, high, _, _ = spec_ref.shape
    _, per, _, row_count, width = held.shape
    sources = row_count // (halves * SUB)
    first = lax.axis_index("real") * sources
    lane = lax.broadcasted_iota(jnp.int32, (2 * row_count, 2 * sides * FT), 1)
    band = (lane % FT) // FB

    def gathered(side, j, at, count):
        parts_of = [
            spec_ref[side, h, at, j].astype(jnp.float32).reshape(count, 2, SUB, FT)
            for h in range(halves)
        ]
        return [
            jnp.stack([p[:, c] for p in parts_of], axis=1).reshape(count * halves * SUB, FT).astype(HALF)
            for c in range(2)
        ]

    def out_copy(j):
        return pltpu.make_async_copy(held.at[j], out_ref.at[pl.ds(j * per, per)], sems.at[j])

    def one_high(j, carry):
        cols, rows_re, rows_im = [], [], []
        for side in range(sides):
            re, im = gathered(side, j, pl.ds(0, parts), parts)
            own_re, own_im = gathered(side, j, pl.ds(first, sources), sources)
            cols += [re, im]
            rows_re += [own_re, own_im]
            rows_im += [own_im, -own_re]
        cols = jnp.concatenate(cols, axis=1)
        rows = jnp.concatenate(
            [jnp.concatenate(rows_re, axis=1), jnp.concatenate(rows_im, axis=1)], axis=0
        )
        for g in range(per):
            kept = jnp.where(band == g, rows, jnp.zeros_like(rows))
            out = lax.dot_general(
                kept, cols, (((1,), (1,)), ((), ())), preferred_element_type=jnp.float32
            )
            held[j, g] = (out * scale).reshape(2, row_count, width)
        out_copy(j).start()
        return carry

    lax.fori_loop(0, high, one_high, 0)
    for j in range(high):
        out_copy(j).wait()


def gram(spectra, row_count, scale):
    sides, halves, parts, high, _, _ = spectra.shape
    width = parts * halves * SUB
    per = FT // FB
    shape = (per, 2, row_count, width)
    return pl.pallas_call(
        functools.partial(gram_kernel, scale),
        out_shape=jax.ShapeDtypeStruct((high * per,) + shape[1:], jnp.float32),
        in_specs=[pl.BlockSpec(memory_space=VMEM)],
        out_specs=pl.BlockSpec(memory_space=ANY),
        scratch_shapes=[VMEM((high,) + shape, jnp.float32), pltpu.SemaphoreType.DMA((high,))],
        compiler_params=pltpu.CompilerParams(vmem_limit_bytes=24 * 1024 * 1024),
    )(spectra)


def tiled_shards(input_field, kerr_coeff, block_list):
    parts, sides = lax.axis_size("mode"), lax.axis_size("real")
    _, _, modes, times = input_field.shape
    width = parts * modes
    spectra = spectra_of(
        input_field.reshape(2, modes, times), kerr_coeff[0], block_list, parts, sides
    )
    return gram(spectra, width // sides, 1.0 / (FB * sides))


def tiles_fit(mesh):
    parts = mesh.shape["mode"]
    return FT % parts == 0 and (2 * FT // parts) % 16 == 0 and mesh.shape["real"] <= 2


def either(mesh, input_field, kerr_coeff, block_list):
    modes = input_field.shape[2]
    blocks_each = kerr_coeff.shape[0]
    fits = tiles_fit(mesh) and modes % 16 == 0 and blocks_each == 1
    fits = fits and input_field.shape[1] == 1 and input_field.shape[3] == NT
    return (tiled_shards if fits else shards)(input_field, kerr_coeff, block_list)


def solution(mesh):
    return jax.shard_map(
        functools.partial(either, mesh),
        mesh=mesh,
        in_specs=(P(None, "real", "mode", None), P("mode", None, None), P("mode", None)),
        out_specs=P("mode", None, "real", None),
        check_vma=False,
    )
```

```python
import functools
import math

import jax
import jax.numpy as jnp
import numpy as np
from jax import lax
from jax.experimental import pallas as pl
from jax.experimental.pallas import tpu as pltpu
from jax.sharding import PartitionSpec as P

MB = 8
FT = 128
NT = 16384
FB = 32


kerr_strength = 0.25


def kerr_terms(field_blocks, coeff_group, block_group):
    mode_l = jnp.take(field_blocks, block_group[:, 1], axis=2).astype(jnp.float32)
    mode_m = jnp.take(field_blocks, block_group[:, 2], axis=2).astype(jnp.float32)
    mode_n = jnp.take(field_blocks, block_group[:, 3], axis=2).astype(jnp.float32)
    realiz = field_blocks.shape[1]
    group_size = block_group.shape[0]
    steps_local = field_blocks.shape[4]
    prod_re = (
        mode_m[0][:, :, :, None, :] * mode_n[0][:, :, None, :, :]
        + mode_m[1][:, :, :, None, :] * mode_n[1][:, :, None, :, :]
    )
    prod_im = (
        mode_m[1][:, :, :, None, :] * mode_n[0][:, :, None, :, :]
        - mode_m[0][:, :, :, None, :] * mode_n[1][:, :, None, :, :]
    )
    pairs = (
        jnp.stack([prod_re, prod_im])
        .reshape(2, realiz, group_size, MB * MB, steps_local)
        .astype(jnp.bfloat16)
    )
    weighted = jnp.einsum(
        "kab,crkbt->crkat", coeff_group, pairs, preferred_element_type=jnp.float32
    )
    weighted = weighted.reshape(2, realiz, group_size, MB, MB, steps_local)
    term_re = jnp.sum(
        weighted[0] * mode_l[0][:, :, None] - weighted[1] * mode_l[1][:, :, None], axis=3
    )
    term_im = jnp.sum(
        weighted[0] * mode_l[1][:, :, None] + weighted[1] * mode_l[0][:, :, None], axis=3
    )
    one_hot = (
        block_group[:, 0][:, None] == jnp.arange(field_blocks.shape[2], dtype=jnp.int32)[None, :]
    ).astype(jnp.float32)
    return jnp.einsum(
        "kg,crkpt->crgpt", one_hot, jnp.stack([term_re, term_im]), precision=lax.Precision.HIGHEST
    )


def phase_table(extent, modulus):
    index_a = jnp.arange(extent, dtype=jnp.int32)[:, None]
    index_b = jnp.arange(extent, dtype=jnp.int32)[None, :]
    angle = 2.0 * math.pi / modulus * (index_a * index_b % modulus).astype(jnp.float32)
    return (jnp.cos(angle), -jnp.sin(angle))


def first_pass(table, data):
    table_high = table.astype(jnp.bfloat16)
    table_low = (table - table_high.astype(jnp.float32)).astype(jnp.bfloat16)
    upper = jnp.einsum("kn,rmnj->rmkj", table_high, data, preferred_element_type=jnp.float32)
    return upper + jnp.einsum("kn,rmnj->rmkj", table_low, data, preferred_element_type=jnp.float32)


def second_pass(table, data):
    return jnp.einsum("jn,rmkn->rmjk", table, data, precision=lax.Precision.HIGH)


def transform(by_mode):
    realiz = by_mode.shape[1]
    local_modes = by_mode.shape[2]
    signal = by_mode.reshape(2, realiz, local_modes, FT, FT)
    four_re, four_im = phase_table(FT, FT)
    twist_re, twist_im = phase_table(FT, NT)
    half_re = first_pass(four_re, signal[0]) - first_pass(four_im, signal[1])
    half_im = first_pass(four_re, signal[1]) + first_pass(four_im, signal[0])
    turned_re = half_re * twist_re - half_im * twist_im
    turned_im = half_re * twist_im + half_im * twist_re
    out_re = (second_pass(four_re, turned_re) - second_pass(four_im, turned_im)) / FT
    out_im = (second_pass(four_re, turned_im) + second_pass(four_im, turned_re)) / FT
    return jnp.stack([out_re, out_im]).astype(jnp.bfloat16)


def gram_parts(rows_part, cols_part):
    mode_parts = jnp.einsum(
        "crpbf,drqbf->bcdpq", rows_part, cols_part, preferred_element_type=jnp.float32
    )
    return jnp.stack(
        [mode_parts[:, 0, 0] + mode_parts[:, 1, 1], mode_parts[:, 1, 0] - mode_parts[:, 0, 1]], axis=1
    )


def shards(input_field, kerr_coeff, block_list):
    timed = lax.all_to_all(input_field, "mode", split_axis=3, concat_axis=2, tiled=True)
    realiz = timed.shape[1]
    width = timed.shape[2]
    steps_local = timed.shape[3]
    field_blocks = timed.reshape(2, realiz, width // MB, MB, steps_local)
    initial = jnp.zeros(field_blocks.shape, jnp.float32)
    running = initial
    coeff_piece = lax.all_gather(kerr_coeff, "mode", axis=0, tiled=True)
    block_piece = lax.all_gather(block_list, "mode", axis=0, tiled=True)
    block_count = block_piece.shape[0]
    coeff_groups = coeff_piece.reshape(
        block_count // 8, 8, coeff_piece.shape[1], coeff_piece.shape[2]
    )
    block_groups = block_piece.reshape(block_count // 8, 8, 4)

    def one_group(carried, groups):
        return (carried + kerr_terms(field_blocks, groups[0], groups[1]), None)

    running, unused = lax.scan(one_group, running, (coeff_groups, block_groups))
    kerr_sum = running
    kerr_sum = kerr_sum.reshape(2, realiz, width, steps_local)
    base = timed.astype(jnp.float32)
    stepped = jnp.stack(
        [base[0] - kerr_strength * kerr_sum[1], base[1] + kerr_strength * kerr_sum[0]]
    ).astype(jnp.bfloat16)
    by_mode = lax.all_to_all(stepped, "mode", split_axis=2, concat_axis=3, tiled=True)
    spectrum = transform(by_mode)
    banded = lax.all_to_all(spectrum, "mode", split_axis=3, concat_axis=2, tiled=True)
    bands_dev = banded.shape[3] * FT // FB
    spec_bands = banded.reshape(2, realiz, width, bands_dev, FB)
    scale = 1.0 / (FB * realiz * lax.axis_size("real"))
    row_count = width // lax.axis_size("real")
    row_first = lax.axis_index("real") * row_count
    shard_piece = lax.all_gather(spec_bands, "real", axis=1, tiled=True)
    own_part = lax.dynamic_slice_in_dim(shard_piece, row_first, row_count, 2)
    return gram_parts(own_part, shard_piece) * scale


VMEM = pltpu.VMEM
ANY = pl.ANY
HALF = jnp.bfloat16
SUB = 8


def plane_size(parts):
    return 4 if parts % 4 == 0 else 1


def partner_order(parts):
    return list(range(1, parts))


def partner(me, step):
    to, bit = me, 1
    while bit <= step:
        if step & bit:
            to = to + bit - 2 * bit * (me // bit % 2)
        bit *= 2
    return to


def remote(here, there, sent, landed, target):
    copy = pltpu.make_async_remote_copy(
        src_ref=here,
        dst_ref=there,
        send_sem=sent,
        recv_sem=landed,
        device_id=target,
        device_id_type=pl.DeviceIdType.MESH,
    )
    copy.start()
    return copy


def local(here, there, sem):
    copy = pltpu.make_async_copy(here, there, sem)
    copy.start()
    return copy


def kerr_terms_of(k, at, list_s, coef, fld, terms):
    piece = fld.shape[3]
    bl, bm, bn = (list_s[*at, 0, i] for i in (1, 2, 3))
    m_re, m_im = fld[0, bm][:, None], fld[1, bm][:, None]
    n_re, n_im = fld[0, bn][None], fld[1, bn][None]
    p_re = (m_re * n_re + m_im * n_im).reshape(MB * MB, piece)
    p_im = (m_im * n_re - m_re * n_im).reshape(MB * MB, piece)
    pairs = jnp.concatenate([p_re, p_im], axis=1).astype(HALF)
    w = jnp.dot(coef, pairs, preferred_element_type=jnp.float32)
    w_re = w[:, :piece].reshape(MB, MB, piece)
    w_im = w[:, piece:].reshape(MB, MB, piece)
    l_re, l_im = fld[0, bl][:, None], fld[1, bl][:, None]
    row = pl.ds(pl.multiple_of(k * MB, MB), MB)
    terms[0, row] = jnp.sum(w_re * l_re - w_im * l_im, axis=0)
    terms[1, row] = jnp.sum(w_re * l_im + w_im * l_re, axis=0)


def owner_table(blocks, width, list_s):
    shape = (width, blocks * MB)
    row = lax.broadcasted_iota(jnp.int32, shape, 0)
    col = lax.broadcasted_iota(jnp.int32, shape, 1)
    wanted = jnp.full(shape, -1, jnp.int32)
    plane = plane_size(blocks)
    for k in range(blocks):
        wanted = jnp.where(col // MB == k, list_s[k % plane, k // plane, 0, 0] * MB + col % MB, wanted)
    return (row == wanted).astype(jnp.float32).astype(HALF)


def swap_rows(coef):
    order_of = (MB * MB, MB * MB)
    row = lax.broadcasted_iota(jnp.int32, order_of, 0)
    col = lax.broadcasted_iota(jnp.int32, order_of, 1)
    swap = (col == (row % MB) * MB + row // MB).astype(jnp.float32).astype(HALF)
    return jnp.dot(swap, coef, preferred_element_type=jnp.float32).astype(HALF)


def pack_coef(coef):
    rows = coef.shape[0] // 2
    return jnp.concatenate([coef[:rows], coef[rows:]], axis=1)


def unpack_coef(packed):
    lanes = packed.shape[1] // 2
    return jnp.concatenate([packed[:, :lanes], packed[:, lanes:]], axis=0)


def whole_kernel(parts, sides, pieces, x_ref, coef_ref, list_ref, *refs):
    table_refs, out_ref = refs[:6], refs[6]
    (timed, coef_in, coef_own, coefs, lists, list_s, fld, terms, stepped, by_mode, xf, rows, spec) = refs[7:20]
    tables, (sends, recvs, own_sems) = refs[20:26], refs[26:]
    me = lax.axis_index("mode")
    other = {"real": 1 - lax.axis_index("real")}
    _, modes, times = x_ref.shape
    steps = times // parts
    width = parts * modes
    groups = width // MB
    half = steps // pieces
    tiles = half // FT
    fine = steps // FT
    halves = modes // SUB
    order = partner_order(parts)
    plane = plane_size(parts)
    barrier = pltpu.get_barrier_semaphore()
    for step in order:
        to = {"mode": partner(me, step)}
        pl.semaphore_signal(barrier, inc=1, device_id=to, device_id_type=pl.DeviceIdType.MESH)
    if sides > 1:
        pl.semaphore_signal(barrier, inc=1, device_id=other, device_id_type=pl.DeviceIdType.MESH)

    local(coef_ref, coef_in, own_sems.at[0]).wait()
    early = [local(a, b, own_sems.at[4 + i]) for i, (a, b) in enumerate(zip(table_refs, tables))]
    coef_own[...] = pack_coef(swap_rows(coef_in[...]))
    pl.semaphore_wait(barrier, parts - 1 + (sides > 1))

    slot = iter(range(sends.shape[0]))
    column, row_of = me % plane, me // plane

    def send_all(here, there, steps_of=order):
        at = next(slot)
        return [
            remote(here(partner(me, step)), there, sends.at[at, step], recvs.at[at, step],
                   {"mode": partner(me, step)})
            for step in steps_of
        ]

    own_coef = coefs.at[column, row_of]
    first = send_all(lambda to: coef_own, own_coef, [step for step in order if step % plane == 0])
    first.append(local(coef_own, own_coef, own_sems.at[0]))
    own_list = lists.at[column, row_of]
    first += send_all(lambda to: list_ref, own_list, [step for step in order if step % plane == 0])
    first.append(local(list_ref, own_list, own_sems.at[1]))

    def chunk(to, part):
        at = pl.multiple_of(to * steps + part * half, FT)
        return x_ref.at[:, :, pl.ds(at, half)]

    def send_field(part):
        copies = send_all(lambda to: chunk(to, part), timed.at[part, me])
        copies.append(local(chunk(me, part), timed.at[part, me], own_sems.at[10 + part]))
        return copies

    field_copies = [send_field(0)]
    for copy in first:
        copy.wait()
    near = [step for step in order if step < plane]
    listed = send_all(lambda to: lists.at[column], lists.at[column], near)
    second = send_all(lambda to: coefs.at[column], coefs.at[column], near)
    field_copies += [send_field(part) for part in range(1, pieces)]
    for copy in listed:
        copy.wait()
    local(lists, list_s, own_sems.at[2]).wait()
    owners = owner_table(parts, width, list_s)
    for copy in second:
        copy.wait()

    mode_copies = [[] for _ in range(halves)]

    def send_stepped(part, h):
        copies = send_all(lambda to: stepped.at[part, h, to], by_mode.at[part, h, me])
        copies.append(
            local(stepped.at[part, h, me], by_mode.at[part, h, me], own_sems.at[20 + part * halves + h])
        )
        mode_copies[h].append((part, copies))

    for part, copies in enumerate(field_copies):
        for copy in copies:
            copy.wait()
        for c in range(2):
            fld[c] = timed[part, :, c].astype(jnp.float32).reshape(groups, MB, half)

        def one_block(k, carry):
            at = (k % plane, k // plane)
            kerr_terms_of(k, at, list_s, unpack_coef(coefs[at]), fld, terms)
            return carry

        lax.fori_loop(0, parts, one_block, 0, unroll=2)
        for c in range(2):
            term = terms[1 - c]
            high = term.astype(HALF)
            low = (term - high.astype(jnp.float32)).astype(HALF)
            kerr = jnp.dot(owners, high, preferred_element_type=jnp.float32)
            kerr = kerr + jnp.dot(owners, low, preferred_element_type=jnp.float32)
            turn = kerr_strength * (2 * c - 1)
            new = fld[c].reshape(width, half) + turn * kerr
            new = new.reshape(parts, halves, SUB, half)
            for h in range(halves):
                stack = [new[:, h, :, n * FT : (n + 1) * FT] for n in range(tiles)]
                stepped[part, h, :, c] = jnp.concatenate(stack, axis=1).astype(HALF)
        send_stepped(part, 0)
    for h in range(1, halves):
        for part in range(pieces):
            send_stepped(part, h)
    for copy in early:
        copy.wait()

    def send_spectra(h):
        copies = send_all(lambda to: spec.at[h, to], out_ref.at[0, h, me])
        own = local(spec.at[h, me], out_ref.at[0, h, me], own_sems.at[3 if h else 0])
        passed = []
        if sides > 1:
            at = next(slot)
            passed.append(remote(spec.at[h, me], out_ref.at[1, h, me], sends.at[at, 0], recvs.at[at, 0], other))
        else:
            at = None
        return copies, own, passed, at

    outgoing = []
    for h in range(halves):
        for part, copies in mode_copies[h]:
            for copy in copies:
                copy.wait()
            for c in range(2):
                for n in range(tiles):
                    xf[c, :, part * tiles + n] = by_mode[
                        part, h, :, c, n * SUB : (n + 1) * SUB
                    ].astype(jnp.float32)
        dft_modes(xf, rows, tables)
        spec[h] = pair_lanes(rows[...]).reshape(spec.shape[1:]).astype(HALF)
        outgoing.append(send_spectra(h))
    for h, (copies, own, passed, at) in enumerate(outgoing):
        for step, copy in zip(order, copies):
            copy.wait_recv()
            if sides > 1:
                source = partner(me, step)
                passed.append(
                    remote(out_ref.at[0, h, source], out_ref.at[1, h, source],
                           sends.at[at, step], recvs.at[at, step], other)
                )
    for copies, own, passed, _ in outgoing:
        own.wait()
        for copy in copies:
            copy.wait_send()
        for copy in passed:
            copy.wait()


def spectra_of(field, coef, listed, parts, sides):
    _, modes, times = field.shape
    steps = times // parts
    width = parts * modes
    fine = steps // FT
    halves = modes // SUB
    pieces = max(fine // 2, 1)
    half = steps // pieces
    tiles = half // FT
    plane = plane_size(parts)
    tables = dft_tables()
    slots = 4 + pieces * (1 + halves) + 2 * halves
    packed = (coef.shape[0] // 2, coef.shape[1] * 2)
    spread = (halves, parts, fine, 2 * SUB, FT)
    return pl.pallas_call(
        functools.partial(whole_kernel, parts, sides, pieces),
        out_shape=jax.ShapeDtypeStruct((sides,) + spread, HALF),
        in_specs=[pl.BlockSpec(memory_space=pltpu.HBM)] * (3 + len(tables)),
        out_specs=pl.BlockSpec(memory_space=ANY),
        scratch_shapes=[
            VMEM((pieces, parts, 2, modes, half), HALF),
            VMEM(coef.shape, HALF),
            VMEM(packed, HALF),
            VMEM((plane, parts // plane) + packed, HALF),
            VMEM((plane, parts // plane) + listed.shape, jnp.int32),
            pltpu.SMEM((plane, parts // plane) + listed.shape, jnp.int32),
            VMEM((2, width // MB, MB, half), jnp.float32),
            VMEM((2, parts * MB, half), jnp.float32),
            VMEM((pieces, halves, parts, 2, tiles * SUB, FT), HALF),
            VMEM((pieces, halves, parts, 2, tiles * SUB, FT), HALF),
            VMEM((2, parts, fine, SUB, FT), jnp.float32),
            VMEM((2 * FT * SUB, FT), jnp.float32),
            VMEM(spread, HALF),
        ]
        + [VMEM(t.shape, t.dtype) for t in tables]
        + [
            pltpu.SemaphoreType.DMA((slots, parts)),
            pltpu.SemaphoreType.DMA((slots, parts)),
            pltpu.SemaphoreType.DMA((20 + pieces * halves,)),
        ],
        compiler_params=pltpu.CompilerParams(
            collective_id=0, has_side_effects=True, vmem_limit_bytes=28 * 1024 * 1024
        ),
    )(*(pltpu.with_memory_space_constraint(a, pltpu.HBM) for a in (field, coef, listed, *tables)))


def dft_tables():
    a = np.arange(FT)
    four = np.exp(-2j * np.pi / FT * (np.outer(a, a) % FT))
    twist = np.exp(-2j * np.pi / NT * (np.outer(a, a) % NT)) / FT
    first = np.block([[four.real, -four.imag], [four.imag, four.real]])
    second = first.reshape(2, FT, 2 * FT).transpose(1, 0, 2).reshape(2 * FT, 2 * FT)

    def split(t):
        t = t.astype(np.float32)
        high = t.astype(HALF)
        return high, (t - high.astype(np.float32)).astype(HALF)

    return (
        *split(first),
        twist.real.astype(np.float32),
        twist.imag.astype(np.float32),
        *split(second),
    )


def dft_modes(xf, rows, tables):
    f1h, f1l, tw_re, tw_im, f2h, f2l = tables
    flat = xf.reshape(2 * FT * SUB, FT)
    nt = (((1,), (1,)), ((), ()))
    dot = functools.partial(jnp.dot, preferred_element_type=jnp.float32)
    dot_nt = functools.partial(
        lax.dot_general, dimension_numbers=nt, preferred_element_type=jnp.float32
    )
    for m in range(0, SUB, 2):
        x = jnp.concatenate(
            [flat[pl.ds(m + i, 2 * FT, stride=SUB), :].astype(HALF) for i in range(2)], axis=1
        )
        half = dot(f1h[...], x) + dot(f1l[...], x)
        turned = []
        for i in range(2):
            h_re, h_im = half[:FT, i * FT : (i + 1) * FT], half[FT:, i * FT : (i + 1) * FT]
            turned.append(
                jnp.concatenate(
                    [
                        h_re * tw_re[...] - h_im * tw_im[...],
                        h_re * tw_im[...] + h_im * tw_re[...],
                    ],
                    axis=1,
                )
            )
        turned = jnp.concatenate(turned, axis=0)
        high = turned.astype(HALF)
        low = (turned - high.astype(jnp.float32)).astype(HALF)
        out = dot_nt(f2h[...], high) + dot_nt(f2h[...], low) + dot_nt(f2l[...], high)
        for i in range(2):
            rows[pl.ds(m + i, 2 * FT, stride=SUB), :] = out[:, i * FT : (i + 1) * FT]


def pair_lanes(rows):
    both = rows.reshape(FT, 2, SUB, FT)
    re, im = both[:, 0], both[:, 1]
    left = lax.broadcasted_iota(jnp.int32, re.shape, 2) < FT // 2
    low = jnp.where(left, re, pltpu.roll(im, FT // 2, 2))
    high = jnp.where(left, pltpu.roll(re, FT // 2, 2), im)
    return jnp.stack([low, high], axis=1)


def gram_kernel(scale, spec_ref, out_ref, held, sems):
    sides, halves, parts, high, _, _ = spec_ref.shape
    _, per, _, row_count, width = held.shape
    sources = row_count // (halves * SUB)
    first = lax.axis_index("real") * sources
    each = per // 2
    lane = lax.broadcasted_iota(jnp.int32, (2 * row_count, sides * FT), 1)
    band = lane % (FT // 2) // FB

    def gathered(side, j, at, count):
        parts_of = [
            spec_ref[side, h, at, j].astype(jnp.float32).reshape(count, 2, SUB, FT)
            for h in range(halves)
        ]
        return [
            jnp.stack([p[:, i] for p in parts_of], axis=1).reshape(count * halves * SUB, FT)
            for i in range(2)
        ]

    def turned(x):
        moved = pltpu.roll(x, FT // 2, 1)
        at = lax.broadcasted_iota(jnp.int32, x.shape, 1)
        return jnp.where(at < FT // 2, moved, -moved)

    def out_copy(j):
        return pltpu.make_async_copy(held.at[j], out_ref.at[pl.ds(j * per, per)], sems.at[j])

    def one_high(j, carry):
        cols = [gathered(side, j, pl.ds(0, parts), parts) for side in range(sides)]
        own = [gathered(side, j, pl.ds(first, sources), sources) for side in range(sides)]
        for i in range(2):
            col = jnp.concatenate([c[i] for c in cols], axis=1).astype(HALF)
            row = jnp.concatenate(
                [
                    jnp.concatenate([o[i] for o in own], axis=1),
                    jnp.concatenate([turned(o[i]) for o in own], axis=1),
                ],
                axis=0,
            ).astype(HALF)
            for g in range(each):
                kept = jnp.where(band == g, row, jnp.zeros_like(row))
                out = lax.dot_general(
                    kept, col, (((1,), (1,)), ((), ())), preferred_element_type=jnp.float32
                )
                held[j, i * each + g] = (out * scale).reshape(2, row_count, width)
        out_copy(j).start()
        return carry

    lax.fori_loop(0, high, one_high, 0)
    for j in range(high):
        out_copy(j).wait()


def gram(spectra, row_count, scale):
    sides, halves, parts, high, _, _ = spectra.shape
    width = parts * halves * SUB
    per = FT // FB
    shape = (per, 2, row_count, width)
    return pl.pallas_call(
        functools.partial(gram_kernel, scale),
        out_shape=jax.ShapeDtypeStruct((high * per,) + shape[1:], jnp.float32),
        in_specs=[pl.BlockSpec(memory_space=VMEM)],
        out_specs=pl.BlockSpec(memory_space=ANY),
        scratch_shapes=[VMEM((high,) + shape, jnp.float32), pltpu.SemaphoreType.DMA((high,))],
        compiler_params=pltpu.CompilerParams(vmem_limit_bytes=24 * 1024 * 1024),
    )(spectra)


def tiled_shards(input_field, kerr_coeff, block_list):
    parts, sides = lax.axis_size("mode"), lax.axis_size("real")
    _, _, modes, times = input_field.shape
    width = parts * modes
    spectra = spectra_of(
        input_field.reshape(2, modes, times), kerr_coeff[0], block_list, parts, sides
    )
    return gram(spectra, width // sides, 1.0 / (FB * sides))


def tiles_fit(mesh):
    parts = mesh.shape["mode"]
    return FT % parts == 0 and (2 * FT // parts) % 16 == 0 and mesh.shape["real"] <= 2


def either(mesh, input_field, kerr_coeff, block_list):
    modes = input_field.shape[2]
    blocks_each = kerr_coeff.shape[0]
    fits = tiles_fit(mesh) and modes % 16 == 0 and blocks_each == 1
    fits = fits and input_field.shape[1] == 1 and input_field.shape[3] == NT
    return (tiled_shards if fits else shards)(input_field, kerr_coeff, block_list)


def solution(mesh):
    return jax.shard_map(
        functools.partial(either, mesh),
        mesh=mesh,
        in_specs=(P(None, "real", "mode", None), P("mode", None, None), P("mode", None)),
        out_specs=P("mode", None, "real", None),
        check_vma=False,
    )
```

```python
import functools
import math

import jax
import jax.numpy as jnp
import numpy as np
from jax import lax
from jax.experimental import pallas as pl
from jax.experimental.pallas import tpu as pltpu
from jax.sharding import PartitionSpec as P

MB = 8
FT = 128
NT = 16384
FB = 32


kerr_strength = 0.25


def kerr_terms(field_blocks, coeff_group, block_group):
    mode_l = jnp.take(field_blocks, block_group[:, 1], axis=2).astype(jnp.float32)
    mode_m = jnp.take(field_blocks, block_group[:, 2], axis=2).astype(jnp.float32)
    mode_n = jnp.take(field_blocks, block_group[:, 3], axis=2).astype(jnp.float32)
    realiz = field_blocks.shape[1]
    group_size = block_group.shape[0]
    steps_local = field_blocks.shape[4]
    prod_re = (
        mode_m[0][:, :, :, None, :] * mode_n[0][:, :, None, :, :]
        + mode_m[1][:, :, :, None, :] * mode_n[1][:, :, None, :, :]
    )
    prod_im = (
        mode_m[1][:, :, :, None, :] * mode_n[0][:, :, None, :, :]
        - mode_m[0][:, :, :, None, :] * mode_n[1][:, :, None, :, :]
    )
    pairs = (
        jnp.stack([prod_re, prod_im])
        .reshape(2, realiz, group_size, MB * MB, steps_local)
        .astype(jnp.bfloat16)
    )
    weighted = jnp.einsum(
        "kab,crkbt->crkat", coeff_group, pairs, preferred_element_type=jnp.float32
    )
    weighted = weighted.reshape(2, realiz, group_size, MB, MB, steps_local)
    term_re = jnp.sum(
        weighted[0] * mode_l[0][:, :, None] - weighted[1] * mode_l[1][:, :, None], axis=3
    )
    term_im = jnp.sum(
        weighted[0] * mode_l[1][:, :, None] + weighted[1] * mode_l[0][:, :, None], axis=3
    )
    one_hot = (
        block_group[:, 0][:, None] == jnp.arange(field_blocks.shape[2], dtype=jnp.int32)[None, :]
    ).astype(jnp.float32)
    return jnp.einsum(
        "kg,crkpt->crgpt", one_hot, jnp.stack([term_re, term_im]), precision=lax.Precision.HIGHEST
    )


def phase_table(extent, modulus):
    index_a = jnp.arange(extent, dtype=jnp.int32)[:, None]
    index_b = jnp.arange(extent, dtype=jnp.int32)[None, :]
    angle = 2.0 * math.pi / modulus * (index_a * index_b % modulus).astype(jnp.float32)
    return (jnp.cos(angle), -jnp.sin(angle))


def first_pass(table, data):
    table_high = table.astype(jnp.bfloat16)
    table_low = (table - table_high.astype(jnp.float32)).astype(jnp.bfloat16)
    upper = jnp.einsum("kn,rmnj->rmkj", table_high, data, preferred_element_type=jnp.float32)
    return upper + jnp.einsum("kn,rmnj->rmkj", table_low, data, preferred_element_type=jnp.float32)


def second_pass(table, data):
    return jnp.einsum("jn,rmkn->rmjk", table, data, precision=lax.Precision.HIGH)


def transform(by_mode):
    realiz = by_mode.shape[1]
    local_modes = by_mode.shape[2]
    signal = by_mode.reshape(2, realiz, local_modes, FT, FT)
    four_re, four_im = phase_table(FT, FT)
    twist_re, twist_im = phase_table(FT, NT)
    half_re = first_pass(four_re, signal[0]) - first_pass(four_im, signal[1])
    half_im = first_pass(four_re, signal[1]) + first_pass(four_im, signal[0])
    turned_re = half_re * twist_re - half_im * twist_im
    turned_im = half_re * twist_im + half_im * twist_re
    out_re = (second_pass(four_re, turned_re) - second_pass(four_im, turned_im)) / FT
    out_im = (second_pass(four_re, turned_im) + second_pass(four_im, turned_re)) / FT
    return jnp.stack([out_re, out_im]).astype(jnp.bfloat16)


def gram_parts(rows_part, cols_part):
    mode_parts = jnp.einsum(
        "crpbf,drqbf->bcdpq", rows_part, cols_part, preferred_element_type=jnp.float32
    )
    return jnp.stack(
        [mode_parts[:, 0, 0] + mode_parts[:, 1, 1], mode_parts[:, 1, 0] - mode_parts[:, 0, 1]], axis=1
    )


def shards(input_field, kerr_coeff, block_list):
    timed = lax.all_to_all(input_field, "mode", split_axis=3, concat_axis=2, tiled=True)
    realiz = timed.shape[1]
    width = timed.shape[2]
    steps_local = timed.shape[3]
    field_blocks = timed.reshape(2, realiz, width // MB, MB, steps_local)
    initial = jnp.zeros(field_blocks.shape, jnp.float32)
    running = initial
    coeff_piece = lax.all_gather(kerr_coeff, "mode", axis=0, tiled=True)
    block_piece = lax.all_gather(block_list, "mode", axis=0, tiled=True)
    block_count = block_piece.shape[0]
    coeff_groups = coeff_piece.reshape(
        block_count // 8, 8, coeff_piece.shape[1], coeff_piece.shape[2]
    )
    block_groups = block_piece.reshape(block_count // 8, 8, 4)

    def one_group(carried, groups):
        return (carried + kerr_terms(field_blocks, groups[0], groups[1]), None)

    running, unused = lax.scan(one_group, running, (coeff_groups, block_groups))
    kerr_sum = running
    kerr_sum = kerr_sum.reshape(2, realiz, width, steps_local)
    base = timed.astype(jnp.float32)
    stepped = jnp.stack(
        [base[0] - kerr_strength * kerr_sum[1], base[1] + kerr_strength * kerr_sum[0]]
    ).astype(jnp.bfloat16)
    by_mode = lax.all_to_all(stepped, "mode", split_axis=2, concat_axis=3, tiled=True)
    spectrum = transform(by_mode)
    banded = lax.all_to_all(spectrum, "mode", split_axis=3, concat_axis=2, tiled=True)
    bands_dev = banded.shape[3] * FT // FB
    spec_bands = banded.reshape(2, realiz, width, bands_dev, FB)
    scale = 1.0 / (FB * realiz * lax.axis_size("real"))
    row_count = width // lax.axis_size("real")
    row_first = lax.axis_index("real") * row_count
    shard_piece = lax.all_gather(spec_bands, "real", axis=1, tiled=True)
    own_part = lax.dynamic_slice_in_dim(shard_piece, row_first, row_count, 2)
    return gram_parts(own_part, shard_piece) * scale


VMEM = pltpu.VMEM
ANY = pl.ANY
HALF = jnp.bfloat16
SUB = 8


def plane_size(parts):
    return 4 if parts % 4 == 0 else 1


def partner_order(parts):
    return list(range(1, parts))


def partner(me, step):
    to, bit = me, 1
    while bit <= step:
        if step & bit:
            to = to + bit - 2 * bit * (me // bit % 2)
        bit *= 2
    return to


def remote(here, there, sent, landed, target):
    copy = pltpu.make_async_remote_copy(
        src_ref=here,
        dst_ref=there,
        send_sem=sent,
        recv_sem=landed,
        device_id=target,
        device_id_type=pl.DeviceIdType.MESH,
    )
    copy.start()
    return copy


def local(here, there, sem):
    copy = pltpu.make_async_copy(here, there, sem)
    copy.start()
    return copy


def kerr_terms_of(k, at, piece, list_s, coef, fld, terms):
    span = pl.ds(0, piece)
    bl, bm, bn = (list_s[*at, 0, i] for i in (1, 2, 3))
    m_re, m_im = fld[0, bm, :, span][:, None], fld[1, bm, :, span][:, None]
    n_re, n_im = fld[0, bn, :, span][None], fld[1, bn, :, span][None]
    p_re = (m_re * n_re + m_im * n_im).reshape(MB * MB, piece)
    p_im = (m_im * n_re - m_re * n_im).reshape(MB * MB, piece)
    pairs = jnp.concatenate([p_re, p_im], axis=1).astype(HALF)
    w = jnp.dot(coef, pairs, preferred_element_type=jnp.float32)
    w_re = w[:, :piece].reshape(MB, MB, piece)
    w_im = w[:, piece:].reshape(MB, MB, piece)
    l_re, l_im = fld[0, bl, :, span][:, None], fld[1, bl, :, span][:, None]
    row = pl.ds(pl.multiple_of(k * MB, MB), MB)
    terms[0, row, span] = jnp.sum(w_re * l_re - w_im * l_im, axis=0)
    terms[1, row, span] = jnp.sum(w_re * l_im + w_im * l_re, axis=0)


def owner_table(blocks, width, list_s):
    shape = (width, blocks * MB)
    row = lax.broadcasted_iota(jnp.int32, shape, 0)
    col = lax.broadcasted_iota(jnp.int32, shape, 1)
    wanted = jnp.full(shape, -1, jnp.int32)
    plane = plane_size(blocks)
    for k in range(blocks):
        wanted = jnp.where(col // MB == k, list_s[k % plane, k // plane, 0, 0] * MB + col % MB, wanted)
    return (row == wanted).astype(jnp.float32).astype(HALF)


def swap_rows(coef):
    order_of = (MB * MB, MB * MB)
    row = lax.broadcasted_iota(jnp.int32, order_of, 0)
    col = lax.broadcasted_iota(jnp.int32, order_of, 1)
    swap = (col == (row % MB) * MB + row // MB).astype(jnp.float32).astype(HALF)
    return jnp.dot(swap, coef, preferred_element_type=jnp.float32).astype(HALF)


def pack_coef(coef):
    rows = coef.shape[0] // 2
    return jnp.concatenate([coef[:rows], coef[rows:]], axis=1)


def unpack_coef(pieces):
    packed = jnp.concatenate(pieces, axis=0)
    lanes = packed.shape[1] // 2
    return jnp.concatenate([packed[:, :lanes], packed[:, lanes:]], axis=0)


def whole_kernel(parts, sides, cuts, x_ref, coef_ref, list_ref, *refs):
    table_refs, out_ref = refs[:6], refs[6]
    (timed, coef_in, coef_own, coefs, lists, list_s, fld, terms, stepped, by_mode, xf, rows, spec) = refs[7:20]
    tables, (sends, recvs, own_sems) = refs[20:26], refs[26:]
    me = lax.axis_index("mode")
    other = {"real": 1 - lax.axis_index("real")}
    _, modes, times = x_ref.shape
    steps = times // parts
    width = parts * modes
    groups = width // MB
    fine = steps // FT
    pieces = len(cuts)
    starts = [sum(cuts[:part]) for part in range(pieces)]
    halves = modes // SUB
    order = partner_order(parts)
    plane = plane_size(parts)
    barrier = pltpu.get_barrier_semaphore()
    for step in order:
        to = {"mode": partner(me, step)}
        pl.semaphore_signal(barrier, inc=1, device_id=to, device_id_type=pl.DeviceIdType.MESH)
    if sides > 1:
        pl.semaphore_signal(barrier, inc=1, device_id=other, device_id_type=pl.DeviceIdType.MESH)

    local(coef_ref, coef_in, own_sems.at[0]).wait()
    early = [local(a, b, own_sems.at[4 + i]) for i, (a, b) in enumerate(zip(table_refs, tables))]
    coef_own[...] = pack_coef(swap_rows(coef_in[...])).reshape(coef_own.shape)
    pl.semaphore_wait(barrier, parts - 1 + (sides > 1))

    slot = iter(range(sends.shape[0]))
    column, row_of = me % plane, me // plane

    def send_all(here, there, steps_of=order):
        at = next(slot)
        return [
            remote(here(partner(me, step)), there, sends.at[at, step], recvs.at[at, step],
                   {"mode": partner(me, step)})
            for step in steps_of
        ]

    side = lax.axis_index("real")
    own_coef = coefs.at[side, column, row_of]
    mine = coef_own.at[side]
    first = send_all(lambda to: mine, own_coef, [step for step in order if step % plane == 0])
    first.append(local(mine, own_coef, own_sems.at[0]))
    own_list = lists.at[column, row_of]
    first += send_all(lambda to: list_ref, own_list, [step for step in order if step % plane == 0])
    first.append(local(list_ref, own_list, own_sems.at[1]))

    def chunk(to, part):
        at = pl.multiple_of(to * steps + starts[part] * FT, FT)
        return x_ref.at[:, :, pl.ds(at, cuts[part] * FT)]

    def landing(part):
        return timed.at[me, :, :, pl.ds(starts[part] * FT, cuts[part] * FT)]

    def send_field(part):
        copies = send_all(lambda to: chunk(to, part), landing(part))
        copies.append(local(chunk(me, part), landing(part), own_sems.at[10 + part]))
        return copies

    field_copies = [send_field(0)]
    for copy in first:
        copy.wait()
    near = [step for step in order if step < plane]
    listed = send_all(lambda to: lists.at[column], lists.at[column], near)
    second = send_all(lambda to: coefs.at[side, column], coefs.at[side, column], near)
    field_copies += [send_field(part) for part in range(1, pieces)]
    for copy in listed:
        copy.wait()
    local(lists, list_s, own_sems.at[2]).wait()
    owners = owner_table(parts, width, list_s)
    for copy in second:
        copy.wait()
    if sides > 1:
        at = next(slot)
        remote(coefs.at[side], coefs.at[side], sends.at[at, 0], recvs.at[at, 0], other).wait()

    mode_copies = [[] for _ in range(halves)]

    def send_stepped(h, first_tile, tiles):
        some = pl.ds(first_tile // 2, tiles // 2)
        copies = send_all(lambda to: stepped.at[h, to, some], by_mode.at[h, me, some])
        at = own_sems.at[20 + halves * pieces + h if tiles == fine else 20 + h * pieces + starts.index(first_tile)]
        copies.append(local(stepped.at[h, me, some], by_mode.at[h, me, some], at))
        mode_copies[h].append((first_tile, tiles, copies))

    for part, copies in enumerate(field_copies):
        for copy in copies:
            copy.wait()
        tiles = cuts[part]
        half = tiles * FT
        here, span = pl.ds(0, half), pl.ds(starts[part] * FT, half)
        for c in range(2):
            fld[c, :, :, here] = timed[:, c, :, span].astype(jnp.float32).reshape(groups, MB, half)

        def one_block(k, carry):
            at = (k % plane, k // plane)
            coef = unpack_coef([coefs[i, *at] for i in range(sides)])
            kerr_terms_of(k, at, half, list_s, coef, fld, terms)
            return carry

        lax.fori_loop(0, parts, one_block, 0, unroll=2)
        for c in range(2):
            term = terms[1 - c, :, here]
            high = term.astype(HALF)
            low = (term - high.astype(jnp.float32)).astype(HALF)
            kerr = jnp.dot(owners, high, preferred_element_type=jnp.float32)
            kerr = kerr + jnp.dot(owners, low, preferred_element_type=jnp.float32)
            turn = kerr_strength * (2 * c - 1)
            new = fld[c, :, :, here].reshape(width, half) + turn * kerr
            new = new.reshape(parts, halves, SUB, half)
            for h in range(halves):
                for n in range(0, tiles, 2):
                    pair = [new[:, h, :, (n + i) * FT : (n + i + 1) * FT] for i in range(2)]
                    stepped[h, :, (starts[part] + n) // 2, c] = jnp.concatenate(pair, axis=1).astype(HALF)
        send_stepped(0, starts[part], tiles)
    for h in range(1, halves):
        send_stepped(h, 0, fine)
    for copy in early:
        copy.wait()

    def is_zero(number):
        return (parts - number) // parts

    def first_device_first():
        pairs = []
        for step in order:
            if step == order[0]:
                other_way = is_zero(me)
                pairs.append((other_way, me + other_way))
            else:
                same = is_zero((me - step + parts) % parts)
                pairs.append(
                    (
                        partner(me, step) * (1 - same) + partner(me, order[0]) * same,
                        step * (1 - same) + order[0] * same,
                    )
                )
        return pairs


    def send_spectra(h):
        listed_targets = first_device_first()
        at = next(slot)
        copies = [
            (
                remote(spec.at[h, to], out_ref.at[0, h, me], sends.at[at, step], recvs.at[at, step], {"mode": to}),
                to,
                step,
            )
            for to, step in listed_targets
        ]
        own = local(spec.at[h, me], out_ref.at[0, h, me], own_sems.at[3 if h else 0])
        passed = []
        if sides > 1:
            at = next(slot)
            passed.append(remote(spec.at[h, me], out_ref.at[1, h, me], sends.at[at, 0], recvs.at[at, 0], other))
        else:
            at = None
        return copies, own, passed, at

    outgoing = []
    for h in range(halves):
        for first_tile, tiles, copies in mode_copies[h]:
            for copy in copies:
                copy.wait()
            for n in range(first_tile, first_tile + tiles, 2):
                for c in range(2):
                    pair = by_mode[h, :, n // 2, c].astype(jnp.float32)
                    xf[c, :, n : n + 2] = pair.reshape(parts, 2, SUB, FT)
        dft_modes(xf, rows, tables)
        spec[h] = pair_lanes(rows[...]).reshape(spec.shape[1:]).astype(HALF)
        outgoing.append(send_spectra(h))
    for h, (copies, own, passed, at) in enumerate(outgoing):
        for copy, source, step in copies:
            copy.wait_recv()
            if sides > 1:
                passed.append(
                    remote(out_ref.at[0, h, source], out_ref.at[1, h, source],
                           sends.at[at, step], recvs.at[at, step], other)
                )
    for copies, own, passed, _ in outgoing:
        own.wait()
        for copy, _, _ in copies:
            copy.wait_send()
        for copy in passed:
            copy.wait()


def spectra_of(field, coef, listed, parts, sides):
    _, modes, times = field.shape
    steps = times // parts
    width = parts * modes
    fine = steps // FT
    halves = modes // SUB
    cuts = [fine // 2, fine // 2]
    pieces = len(cuts)
    half = max(cuts) * FT
    plane = plane_size(parts)
    tables = dft_tables()
    slots = 5 + pieces * 2 + 3 * halves
    packed = (coef.shape[0] // 2 // sides, coef.shape[1] * 2)
    spread = (halves, parts, fine, 2 * SUB, FT)
    return pl.pallas_call(
        functools.partial(whole_kernel, parts, sides, cuts),
        out_shape=jax.ShapeDtypeStruct((sides,) + spread, HALF),
        in_specs=[pl.BlockSpec(memory_space=pltpu.HBM)] * (3 + len(tables)),
        out_specs=pl.BlockSpec(memory_space=ANY),
        scratch_shapes=[
            VMEM((parts, 2, modes, steps), HALF),
            VMEM(coef.shape, HALF),
            VMEM((sides,) + packed, HALF),
            VMEM((sides, plane, parts // plane) + packed, HALF),
            VMEM((plane, parts // plane) + listed.shape, jnp.int32),
            pltpu.SMEM((plane, parts // plane) + listed.shape, jnp.int32),
            VMEM((2, width // MB, MB, half), jnp.float32),
            VMEM((2, parts * MB, half), jnp.float32),
            VMEM((halves, parts, fine // 2, 2, 2 * SUB, FT), HALF),
            VMEM((halves, parts, fine // 2, 2, 2 * SUB, FT), HALF),
            VMEM((2, parts, fine, SUB, FT), jnp.float32),
            VMEM((2 * FT * SUB, FT), jnp.float32),
            VMEM(spread, HALF),
        ]
        + [VMEM(t.shape, t.dtype) for t in tables]
        + [
            pltpu.SemaphoreType.DMA((slots, parts)),
            pltpu.SemaphoreType.DMA((slots, parts)),
            pltpu.SemaphoreType.DMA((20 + (pieces + 1) * halves,)),
        ],
        compiler_params=pltpu.CompilerParams(
            collective_id=0, has_side_effects=True, vmem_limit_bytes=28 * 1024 * 1024
        ),
    )(*(pltpu.with_memory_space_constraint(a, pltpu.HBM) for a in (field, coef, listed, *tables)))


def dft_tables():
    a = np.arange(FT)
    four = np.exp(-2j * np.pi / FT * (np.outer(a, a) % FT))
    twist = np.exp(-2j * np.pi / NT * (np.outer(a, a) % NT)) / FT
    first = np.block([[four.real, -four.imag], [four.imag, four.real]])
    second = first.reshape(2, FT, 2 * FT).transpose(1, 0, 2).reshape(2 * FT, 2 * FT)

    def split(t):
        t = t.astype(np.float32)
        high = t.astype(HALF)
        return high, (t - high.astype(np.float32)).astype(HALF)

    return (
        *split(first),
        twist.real.astype(np.float32),
        twist.imag.astype(np.float32),
        *split(second),
    )


def dft_modes(xf, rows, tables):
    f1h, f1l, tw_re, tw_im, f2h, f2l = tables
    flat = xf.reshape(2 * FT * SUB, FT)
    nt = (((1,), (1,)), ((), ()))
    dot = functools.partial(jnp.dot, preferred_element_type=jnp.float32)
    dot_nt = functools.partial(
        lax.dot_general, dimension_numbers=nt, preferred_element_type=jnp.float32
    )
    for m in range(0, SUB, 2):
        x = jnp.concatenate(
            [flat[pl.ds(m + i, 2 * FT, stride=SUB), :].astype(HALF) for i in range(2)], axis=1
        )
        half = dot(f1h[...], x) + dot(f1l[...], x)
        turned = []
        for i in range(2):
            h_re, h_im = half[:FT, i * FT : (i + 1) * FT], half[FT:, i * FT : (i + 1) * FT]
            turned.append(
                jnp.concatenate(
                    [
                        h_re * tw_re[...] - h_im * tw_im[...],
                        h_re * tw_im[...] + h_im * tw_re[...],
                    ],
                    axis=1,
                )
            )
        turned = jnp.concatenate(turned, axis=0)
        high = turned.astype(HALF)
        low = (turned - high.astype(jnp.float32)).astype(HALF)
        out = dot_nt(f2h[...], high) + dot_nt(f2h[...], low) + dot_nt(f2l[...], high)
        for i in range(2):
            rows[pl.ds(m + i, 2 * FT, stride=SUB), :] = out[:, i * FT : (i + 1) * FT]


def pair_lanes(rows):
    both = rows.reshape(FT, 2, SUB, FT)
    re, im = both[:, 0], both[:, 1]
    left = lax.broadcasted_iota(jnp.int32, re.shape, 2) < FT // 2
    low = jnp.where(left, re, pltpu.roll(im, FT // 2, 2))
    high = jnp.where(left, pltpu.roll(re, FT // 2, 2), im)
    return jnp.stack([low, high], axis=1)


def gram_kernel(scale, spec_ref, out_ref, held, sems):
    sides, halves, parts, high, _, _ = spec_ref.shape
    _, per, _, row_count, width = held.shape
    sources = row_count // (halves * SUB)
    first = lax.axis_index("real") * sources
    each = per // 2
    lane = lax.broadcasted_iota(jnp.int32, (2 * row_count, sides * FT), 1)
    band = lane % (FT // 2) // FB

    def gathered(side, j, at, count):
        parts_of = [
            spec_ref[side, h, at, j].astype(jnp.float32).reshape(count, 2, SUB, FT)
            for h in range(halves)
        ]
        return [
            jnp.stack([p[:, i] for p in parts_of], axis=1).reshape(count * halves * SUB, FT)
            for i in range(2)
        ]

    def turned(x):
        moved = pltpu.roll(x, FT // 2, 1)
        at = lax.broadcasted_iota(jnp.int32, x.shape, 1)
        return jnp.where(at < FT // 2, moved, -moved)

    def out_copy(j):
        return pltpu.make_async_copy(held.at[j], out_ref.at[pl.ds(j * per, per)], sems.at[j])

    def one_high(j, carry):
        cols = [gathered(side, j, pl.ds(0, parts), parts) for side in range(sides)]
        own = [gathered(side, j, pl.ds(first, sources), sources) for side in range(sides)]
        for i in range(2):
            col = jnp.concatenate([c[i] for c in cols], axis=1).astype(HALF)
            row = jnp.concatenate(
                [
                    jnp.concatenate([o[i] for o in own], axis=1),
                    jnp.concatenate([turned(o[i]) for o in own], axis=1),
                ],
                axis=0,
            ).astype(HALF)
            for g in range(each):
                kept = jnp.where(band == g, row, jnp.zeros_like(row))
                out = lax.dot_general(
                    kept, col, (((1,), (1,)), ((), ())), preferred_element_type=jnp.float32
                )
                held[j, i * each + g] = (out * scale).reshape(2, row_count, width)
        out_copy(j).start()
        return carry

    lax.fori_loop(0, high, one_high, 0)
    for j in range(high):
        out_copy(j).wait()


def gram(spectra, row_count, scale):
    sides, halves, parts, high, _, _ = spectra.shape
    width = parts * halves * SUB
    per = FT // FB
    shape = (per, 2, row_count, width)
    return pl.pallas_call(
        functools.partial(gram_kernel, scale),
        out_shape=jax.ShapeDtypeStruct((high * per,) + shape[1:], jnp.float32),
        in_specs=[pl.BlockSpec(memory_space=VMEM)],
        out_specs=pl.BlockSpec(memory_space=ANY),
        scratch_shapes=[VMEM((high,) + shape, jnp.float32), pltpu.SemaphoreType.DMA((high,))],
        compiler_params=pltpu.CompilerParams(vmem_limit_bytes=24 * 1024 * 1024),
    )(spectra)


def tiled_shards(input_field, kerr_coeff, block_list):
    parts, sides = lax.axis_size("mode"), lax.axis_size("real")
    _, _, modes, times = input_field.shape
    width = parts * modes
    spectra = spectra_of(
        input_field.reshape(2, modes, times), kerr_coeff[0], block_list, parts, sides
    )
    return gram(spectra, width // sides, 1.0 / (FB * sides))


def tiles_fit(mesh):
    parts = mesh.shape["mode"]
    return FT % parts == 0 and (2 * FT // parts) % 16 == 0 and mesh.shape["real"] <= 2


def either(mesh, input_field, kerr_coeff, block_list):
    modes = input_field.shape[2]
    blocks_each = kerr_coeff.shape[0]
    fits = tiles_fit(mesh) and modes % 16 == 0 and blocks_each == 1
    fits = fits and input_field.shape[1] == 1 and input_field.shape[3] == NT
    return (tiled_shards if fits else shards)(input_field, kerr_coeff, block_list)


def solution(mesh):
    return jax.shard_map(
        functools.partial(either, mesh),
        mesh=mesh,
        in_specs=(P(None, "real", "mode", None), P("mode", None, None), P("mode", None)),
        out_specs=P("mode", None, "real", None),
        check_vma=False,
    )
```

```python
import functools
import math

import jax
import jax.numpy as jnp
import numpy as np
from jax import lax
from jax.experimental import pallas as pl
from jax.experimental.pallas import tpu as pltpu
from jax.sharding import PartitionSpec as P

MB = 8
FT = 128
NT = 16384
FB = 32


kerr_strength = 0.25


def kerr_terms(field_blocks, coeff_group, block_group):
    mode_l = jnp.take(field_blocks, block_group[:, 1], axis=2).astype(jnp.float32)
    mode_m = jnp.take(field_blocks, block_group[:, 2], axis=2).astype(jnp.float32)
    mode_n = jnp.take(field_blocks, block_group[:, 3], axis=2).astype(jnp.float32)
    realiz = field_blocks.shape[1]
    group_size = block_group.shape[0]
    steps_local = field_blocks.shape[4]
    prod_re = (
        mode_m[0][:, :, :, None, :] * mode_n[0][:, :, None, :, :]
        + mode_m[1][:, :, :, None, :] * mode_n[1][:, :, None, :, :]
    )
    prod_im = (
        mode_m[1][:, :, :, None, :] * mode_n[0][:, :, None, :, :]
        - mode_m[0][:, :, :, None, :] * mode_n[1][:, :, None, :, :]
    )
    pairs = (
        jnp.stack([prod_re, prod_im])
        .reshape(2, realiz, group_size, MB * MB, steps_local)
        .astype(jnp.bfloat16)
    )
    weighted = jnp.einsum(
        "kab,crkbt->crkat", coeff_group, pairs, preferred_element_type=jnp.float32
    )
    weighted = weighted.reshape(2, realiz, group_size, MB, MB, steps_local)
    term_re = jnp.sum(
        weighted[0] * mode_l[0][:, :, None] - weighted[1] * mode_l[1][:, :, None], axis=3
    )
    term_im = jnp.sum(
        weighted[0] * mode_l[1][:, :, None] + weighted[1] * mode_l[0][:, :, None], axis=3
    )
    one_hot = (
        block_group[:, 0][:, None] == jnp.arange(field_blocks.shape[2], dtype=jnp.int32)[None, :]
    ).astype(jnp.float32)
    return jnp.einsum(
        "kg,crkpt->crgpt", one_hot, jnp.stack([term_re, term_im]), precision=lax.Precision.HIGHEST
    )


def phase_table(extent, modulus):
    index_a = jnp.arange(extent, dtype=jnp.int32)[:, None]
    index_b = jnp.arange(extent, dtype=jnp.int32)[None, :]
    angle = 2.0 * math.pi / modulus * (index_a * index_b % modulus).astype(jnp.float32)
    return (jnp.cos(angle), -jnp.sin(angle))


def first_pass(table, data):
    table_high = table.astype(jnp.bfloat16)
    table_low = (table - table_high.astype(jnp.float32)).astype(jnp.bfloat16)
    upper = jnp.einsum("kn,rmnj->rmkj", table_high, data, preferred_element_type=jnp.float32)
    return upper + jnp.einsum("kn,rmnj->rmkj", table_low, data, preferred_element_type=jnp.float32)


def second_pass(table, data):
    return jnp.einsum("jn,rmkn->rmjk", table, data, precision=lax.Precision.HIGH)


def transform(by_mode):
    realiz = by_mode.shape[1]
    local_modes = by_mode.shape[2]
    signal = by_mode.reshape(2, realiz, local_modes, FT, FT)
    four_re, four_im = phase_table(FT, FT)
    twist_re, twist_im = phase_table(FT, NT)
    half_re = first_pass(four_re, signal[0]) - first_pass(four_im, signal[1])
    half_im = first_pass(four_re, signal[1]) + first_pass(four_im, signal[0])
    turned_re = half_re * twist_re - half_im * twist_im
    turned_im = half_re * twist_im + half_im * twist_re
    out_re = (second_pass(four_re, turned_re) - second_pass(four_im, turned_im)) / FT
    out_im = (second_pass(four_re, turned_im) + second_pass(four_im, turned_re)) / FT
    return jnp.stack([out_re, out_im]).astype(jnp.bfloat16)


def gram_parts(rows_part, cols_part):
    mode_parts = jnp.einsum(
        "crpbf,drqbf->bcdpq", rows_part, cols_part, preferred_element_type=jnp.float32
    )
    return jnp.stack(
        [mode_parts[:, 0, 0] + mode_parts[:, 1, 1], mode_parts[:, 1, 0] - mode_parts[:, 0, 1]], axis=1
    )


def shards(input_field, kerr_coeff, block_list):
    timed = lax.all_to_all(input_field, "mode", split_axis=3, concat_axis=2, tiled=True)
    realiz = timed.shape[1]
    width = timed.shape[2]
    steps_local = timed.shape[3]
    field_blocks = timed.reshape(2, realiz, width // MB, MB, steps_local)
    initial = jnp.zeros(field_blocks.shape, jnp.float32)
    running = initial
    coeff_piece = lax.all_gather(kerr_coeff, "mode", axis=0, tiled=True)
    block_piece = lax.all_gather(block_list, "mode", axis=0, tiled=True)
    block_count = block_piece.shape[0]
    coeff_groups = coeff_piece.reshape(
        block_count // 8, 8, coeff_piece.shape[1], coeff_piece.shape[2]
    )
    block_groups = block_piece.reshape(block_count // 8, 8, 4)

    def one_group(carried, groups):
        return (carried + kerr_terms(field_blocks, groups[0], groups[1]), None)

    running, unused = lax.scan(one_group, running, (coeff_groups, block_groups))
    kerr_sum = running
    kerr_sum = kerr_sum.reshape(2, realiz, width, steps_local)
    base = timed.astype(jnp.float32)
    stepped = jnp.stack(
        [base[0] - kerr_strength * kerr_sum[1], base[1] + kerr_strength * kerr_sum[0]]
    ).astype(jnp.bfloat16)
    by_mode = lax.all_to_all(stepped, "mode", split_axis=2, concat_axis=3, tiled=True)
    spectrum = transform(by_mode)
    banded = lax.all_to_all(spectrum, "mode", split_axis=3, concat_axis=2, tiled=True)
    bands_dev = banded.shape[3] * FT // FB
    spec_bands = banded.reshape(2, realiz, width, bands_dev, FB)
    scale = 1.0 / (FB * realiz * lax.axis_size("real"))
    row_count = width // lax.axis_size("real")
    row_first = lax.axis_index("real") * row_count
    shard_piece = lax.all_gather(spec_bands, "real", axis=1, tiled=True)
    own_part = lax.dynamic_slice_in_dim(shard_piece, row_first, row_count, 2)
    return gram_parts(own_part, shard_piece) * scale


VMEM = pltpu.VMEM
ANY = pl.ANY
HALF = jnp.bfloat16
SUB = 8


def plane_size(parts):
    return 4 if parts % 4 == 0 else 1


def partner_order(parts):
    return list(range(1, parts))


def partner(me, step):
    to, bit = me, 1
    while bit <= step:
        if step & bit:
            to = to + bit - 2 * bit * (me // bit % 2)
        bit *= 2
    return to


def remote(here, there, sent, landed, target):
    copy = pltpu.make_async_remote_copy(
        src_ref=here,
        dst_ref=there,
        send_sem=sent,
        recv_sem=landed,
        device_id=target,
        device_id_type=pl.DeviceIdType.MESH,
    )
    copy.start()
    return copy


def local(here, there, sem):
    copy = pltpu.make_async_copy(here, there, sem)
    copy.start()
    return copy


def kerr_terms_of(k, at, piece, list_s, coef, fld, terms):
    span = pl.ds(0, piece)
    bl, bm, bn = (list_s[*at, 0, i] for i in (1, 2, 3))
    m_re, m_im = fld[0, bm, :, span][:, None], fld[1, bm, :, span][:, None]
    n_re, n_im = fld[0, bn, :, span][None], fld[1, bn, :, span][None]
    p_re = (m_re * n_re + m_im * n_im).reshape(MB * MB, piece)
    p_im = (m_im * n_re - m_re * n_im).reshape(MB * MB, piece)
    pairs = jnp.concatenate([p_re, p_im], axis=1).astype(HALF)
    w = jnp.dot(coef, pairs, preferred_element_type=jnp.float32)
    w_re = w[:, :piece].reshape(MB, MB, piece)
    w_im = w[:, piece:].reshape(MB, MB, piece)
    l_re, l_im = fld[0, bl, :, span][:, None], fld[1, bl, :, span][:, None]
    row = pl.ds(pl.multiple_of(k * MB, MB), MB)
    terms[0, row, span] = jnp.sum(w_re * l_re - w_im * l_im, axis=0)
    terms[1, row, span] = jnp.sum(w_re * l_im + w_im * l_re, axis=0)


def owner_table(blocks, width, list_s):
    shape = (width, blocks * MB)
    row = lax.broadcasted_iota(jnp.int32, shape, 0)
    col = lax.broadcasted_iota(jnp.int32, shape, 1)
    wanted = jnp.full(shape, -1, jnp.int32)
    plane = plane_size(blocks)
    for k in range(blocks):
        wanted = jnp.where(col // MB == k, list_s[k % plane, k // plane, 0, 0] * MB + col % MB, wanted)
    return (row == wanted).astype(jnp.float32).astype(HALF)


def swap_rows(coef):
    order_of = (MB * MB, MB * MB)
    row = lax.broadcasted_iota(jnp.int32, order_of, 0)
    col = lax.broadcasted_iota(jnp.int32, order_of, 1)
    swap = (col == (row % MB) * MB + row // MB).astype(jnp.float32).astype(HALF)
    return jnp.dot(swap, coef, preferred_element_type=jnp.float32).astype(HALF)


def pack_coef(coef):
    rows = coef.shape[0] // 2
    return jnp.concatenate([coef[:rows], coef[rows:]], axis=1)


def unpack_coef(pieces):
    packed = jnp.concatenate(pieces, axis=0)
    lanes = packed.shape[1] // 2
    return jnp.concatenate([packed[:, :lanes], packed[:, lanes:]], axis=0)


def whole_kernel(parts, sides, cuts, x_ref, coef_ref, list_ref, *refs):
    table_refs, out_ref = refs[:6], refs[6]
    (timed, coef_in, coef_own, coefs, lists, list_s, fld, terms, stepped, by_mode, xf, rows, spec) = refs[7:20]
    tables, (sends, recvs, own_sems) = refs[20:26], refs[26:]
    me = lax.axis_index("mode")
    other = {"real": 1 - lax.axis_index("real")}
    _, modes, times = x_ref.shape
    steps = times // parts
    width = parts * modes
    groups = width // MB
    fine = steps // FT
    pieces = len(cuts)
    starts = [sum(cuts[:part]) for part in range(pieces)]
    halves = modes // SUB
    order = partner_order(parts)
    plane = plane_size(parts)
    barrier = pltpu.get_barrier_semaphore()
    for step in reversed(order):
        to = {"mode": partner(me, step)}
        pl.semaphore_signal(barrier, inc=1, device_id=to, device_id_type=pl.DeviceIdType.MESH)
    if sides > 1:
        pl.semaphore_signal(barrier, inc=1, device_id=other, device_id_type=pl.DeviceIdType.MESH)

    local(coef_ref, coef_in, own_sems.at[0]).wait()
    early = [local(a, b, own_sems.at[4 + i]) for i, (a, b) in enumerate(zip(table_refs, tables))]
    coef_own[...] = pack_coef(swap_rows(coef_in[...])).reshape(coef_own.shape)
    pl.semaphore_wait(barrier, parts - 1 + (sides > 1))

    slot = iter(range(sends.shape[0]))
    column, row_of = me % plane, me // plane

    def send_all(here, there, steps_of=order):
        at = next(slot)
        return [
            remote(here(partner(me, step)), there, sends.at[at, step], recvs.at[at, step],
                   {"mode": partner(me, step)})
            for step in steps_of
        ]

    side = lax.axis_index("real")
    own_coef = coefs.at[side, column, row_of]
    mine = coef_own.at[side]
    first = send_all(lambda to: mine, own_coef, [step for step in order if step % plane == 0])
    first.append(local(mine, own_coef, own_sems.at[0]))
    own_list = lists.at[column, row_of]
    first += send_all(lambda to: list_ref, own_list, [step for step in order if step % plane == 0])
    first.append(local(list_ref, own_list, own_sems.at[1]))

    def chunk(to, part):
        at = pl.multiple_of(to * steps + starts[part] * FT, FT)
        return x_ref.at[:, :, pl.ds(at, cuts[part] * FT)]

    def landing(part):
        return timed.at[me, :, :, pl.ds(starts[part] * FT, cuts[part] * FT)]

    def send_field(part):
        copies = send_all(lambda to: chunk(to, part), landing(part))
        copies.append(local(chunk(me, part), landing(part), own_sems.at[10 + part]))
        return copies

    field_copies = [send_field(0)]
    for copy in first:
        copy.wait()
    near = [step for step in order if step < plane]
    listed = send_all(lambda to: lists.at[column], lists.at[column], near)
    second = send_all(lambda to: coefs.at[side, column], coefs.at[side, column], near)
    field_copies += [send_field(part) for part in range(1, pieces)]
    for copy in listed:
        copy.wait()
    local(lists, list_s, own_sems.at[2]).wait()
    owners = owner_table(parts, width, list_s)
    for copy in second:
        copy.wait()
    if sides > 1:
        at = next(slot)
        remote(coefs.at[side], coefs.at[side], sends.at[at, 0], recvs.at[at, 0], other).wait()

    mode_copies = [[] for _ in range(halves)]

    def send_stepped(h, first_tile, tiles):
        some = pl.ds(first_tile // 2, tiles // 2)
        copies = send_all(lambda to: stepped.at[h, to, some], by_mode.at[h, me, some])
        at = own_sems.at[20 + halves * pieces + h if tiles == fine else 20 + h * pieces + starts.index(first_tile)]
        copies.append(local(stepped.at[h, me, some], by_mode.at[h, me, some], at))
        mode_copies[h].append((first_tile, tiles, copies))

    for part, copies in enumerate(field_copies):
        for copy in copies:
            copy.wait()
        tiles = cuts[part]
        half = tiles * FT
        here, span = pl.ds(0, half), pl.ds(starts[part] * FT, half)
        for c in range(2):
            fld[c, :, :, here] = timed[:, c, :, span].astype(jnp.float32).reshape(groups, MB, half)

        def one_block(k, carry):
            at = (k % plane, k // plane)
            coef = unpack_coef([coefs[i, *at] for i in range(sides)])
            kerr_terms_of(k, at, half, list_s, coef, fld, terms)
            return carry

        lax.fori_loop(0, parts, one_block, 0, unroll=2)
        for c in range(2):
            term = terms[1 - c, :, here]
            high = term.astype(HALF)
            low = (term - high.astype(jnp.float32)).astype(HALF)
            kerr = jnp.dot(owners, high, preferred_element_type=jnp.float32)
            kerr = kerr + jnp.dot(owners, low, preferred_element_type=jnp.float32)
            turn = kerr_strength * (2 * c - 1)
            new = fld[c, :, :, here].reshape(width, half) + turn * kerr
            new = new.reshape(parts, halves, SUB, half)
            for h in range(halves):
                for n in range(0, tiles, 2):
                    pair = [new[:, h, :, (n + i) * FT : (n + i + 1) * FT] for i in range(2)]
                    stepped[h, :, (starts[part] + n) // 2, c] = jnp.concatenate(pair, axis=1).astype(HALF)
        send_stepped(0, starts[part], tiles)
    for h in range(1, halves):
        send_stepped(h, 0, fine)
    for copy in early:
        copy.wait()

    def columns_ascending():
        pairs = []
        for i in range(plane - 1):
            to = i + (i - column + plane) // plane
            step, bit = 0, 1
            while bit < plane:
                step = step + (to // bit + column // bit) % 2 * bit
                bit *= 2
            pairs.append((row_of * plane + to, step))
        for r in range(1, parts // plane):
            for k in range(plane):
                row = partner(me, r * plane) // plane
                pairs.append((row * plane + k, r * plane + partner(column, k)))
        return pairs

    targets = columns_ascending()

    def send_spectra(h):
        at = next(slot)
        copies = [
            remote(spec.at[h, to], out_ref.at[0, h, me], sends.at[at, step], recvs.at[at, step], {"mode": to})
            for to, step in targets
        ]
        own = local(spec.at[h, me], out_ref.at[0, h, me], own_sems.at[3 if h else 0])
        return copies, own, at

    def arrived(h, at, step):
        source = partner(me, step)
        pltpu.make_async_remote_copy(
            src_ref=spec.at[h, source],
            dst_ref=out_ref.at[0, h, source],
            send_sem=sends.at[at, step],
            recv_sem=recvs.at[at, step],
            device_id={"mode": source},
            device_id_type=pl.DeviceIdType.MESH,
        ).wait_recv()

    def passing(h, some, at, which):
        if sides == 1:
            return []
        here, there = out_ref.at[0, h, some], out_ref.at[1, h, some]
        return [remote(here, there, sends.at[at, which], recvs.at[at, which], other)]

    outgoing = []
    for h in range(halves):
        for first_tile, tiles, copies in mode_copies[h]:
            for copy in copies:
                copy.wait()
            for n in range(first_tile, first_tile + tiles, 2):
                for c in range(2):
                    pair = by_mode[h, :, n // 2, c].astype(jnp.float32)
                    xf[c, :, n : n + 2] = pair.reshape(parts, 2, SUB, FT)
        dft_modes(xf, rows, tables)
        spec[h] = pair_lanes(rows[...]).reshape(spec.shape[1:]).astype(HALF)
        outgoing.append(send_spectra(h))
    passed = []
    for h, (copies, own, at) in enumerate(outgoing):
        pass_at = next(slot)
        own.wait()
        for r in range(parts // plane):
            row = partner(me, r * plane) // plane
            for step in range(r * plane, (r + 1) * plane):
                if step:
                    arrived(h, at, step)
            if h == halves - 1:
                passed += passing(h, pl.ds(row * plane, plane), pass_at, r)
        if h < halves - 1:
            passed += passing(h, pl.ds(0, parts), pass_at, 0)
    for copies, _, _ in outgoing:
        for copy in copies:
            copy.wait_send()
    for copy in passed:
        copy.wait()


def spectra_of(field, coef, listed, parts, sides):
    _, modes, times = field.shape
    steps = times // parts
    width = parts * modes
    fine = steps // FT
    halves = modes // SUB
    cuts = [fine // 2, fine // 2]
    pieces = len(cuts)
    half = max(cuts) * FT
    plane = plane_size(parts)
    tables = dft_tables()
    slots = 5 + pieces * 2 + 3 * halves
    packed = (coef.shape[0] // 2 // sides, coef.shape[1] * 2)
    spread = (halves, parts, fine, 2 * SUB, FT)
    return pl.pallas_call(
        functools.partial(whole_kernel, parts, sides, cuts),
        out_shape=jax.ShapeDtypeStruct((sides,) + spread, HALF),
        in_specs=[pl.BlockSpec(memory_space=pltpu.HBM)] * (3 + len(tables)),
        out_specs=pl.BlockSpec(memory_space=ANY),
        scratch_shapes=[
            VMEM((parts, 2, modes, steps), HALF),
            VMEM(coef.shape, HALF),
            VMEM((sides,) + packed, HALF),
            VMEM((sides, plane, parts // plane) + packed, HALF),
            VMEM((plane, parts // plane) + listed.shape, jnp.int32),
            pltpu.SMEM((plane, parts // plane) + listed.shape, jnp.int32),
            VMEM((2, width // MB, MB, half), jnp.float32),
            VMEM((2, parts * MB, half), jnp.float32),
            VMEM((halves, parts, fine // 2, 2, 2 * SUB, FT), HALF),
            VMEM((halves, parts, fine // 2, 2, 2 * SUB, FT), HALF),
            VMEM((2, parts, fine, SUB, FT), jnp.float32),
            VMEM((2 * FT * SUB, FT), jnp.float32),
            VMEM(spread, HALF),
        ]
        + [VMEM(t.shape, t.dtype) for t in tables]
        + [
            pltpu.SemaphoreType.DMA((slots, parts)),
            pltpu.SemaphoreType.DMA((slots, parts)),
            pltpu.SemaphoreType.DMA((20 + (pieces + 1) * halves,)),
        ],
        compiler_params=pltpu.CompilerParams(
            collective_id=0, has_side_effects=True, vmem_limit_bytes=28 * 1024 * 1024
        ),
    )(*(pltpu.with_memory_space_constraint(a, pltpu.HBM) for a in (field, coef, listed, *tables)))


def dft_tables():
    a = np.arange(FT)
    four = np.exp(-2j * np.pi / FT * (np.outer(a, a) % FT))
    twist = np.exp(-2j * np.pi / NT * (np.outer(a, a) % NT)) / FT
    first = np.block([[four.real, -four.imag], [four.imag, four.real]])
    second = first.reshape(2, FT, 2 * FT).transpose(1, 0, 2).reshape(2 * FT, 2 * FT)

    def split(t):
        t = t.astype(np.float32)
        high = t.astype(HALF)
        return high, (t - high.astype(np.float32)).astype(HALF)

    return (
        *split(first),
        twist.real.astype(np.float32),
        twist.imag.astype(np.float32),
        *split(second),
    )


def dft_modes(xf, rows, tables):
    f1h, f1l, tw_re, tw_im, f2h, f2l = tables
    flat = xf.reshape(2 * FT * SUB, FT)
    nt = (((1,), (1,)), ((), ()))
    dot = functools.partial(jnp.dot, preferred_element_type=jnp.float32)
    dot_nt = functools.partial(
        lax.dot_general, dimension_numbers=nt, preferred_element_type=jnp.float32
    )
    for m in range(0, SUB, 2):
        x = jnp.concatenate(
            [flat[pl.ds(m + i, 2 * FT, stride=SUB), :].astype(HALF) for i in range(2)], axis=1
        )
        half = dot(f1h[...], x) + dot(f1l[...], x)
        turned = []
        for i in range(2):
            h_re, h_im = half[:FT, i * FT : (i + 1) * FT], half[FT:, i * FT : (i + 1) * FT]
            turned.append(
                jnp.concatenate(
                    [
                        h_re * tw_re[...] - h_im * tw_im[...],
                        h_re * tw_im[...] + h_im * tw_re[...],
                    ],
                    axis=1,
                )
            )
        turned = jnp.concatenate(turned, axis=0)
        high = turned.astype(HALF)
        low = (turned - high.astype(jnp.float32)).astype(HALF)
        out = dot_nt(f2h[...], high) + dot_nt(f2h[...], low) + dot_nt(f2l[...], high)
        for i in range(2):
            rows[pl.ds(m + i, 2 * FT, stride=SUB), :] = out[:, i * FT : (i + 1) * FT]


def pair_lanes(rows):
    both = rows.reshape(FT, 2, SUB, FT)
    re, im = both[:, 0], both[:, 1]
    left = lax.broadcasted_iota(jnp.int32, re.shape, 2) < FT // 2
    low = jnp.where(left, re, pltpu.roll(im, FT // 2, 2))
    high = jnp.where(left, pltpu.roll(re, FT // 2, 2), im)
    return jnp.stack([low, high], axis=1)


def gram_kernel(scale, spec_ref, out_ref, held, sems):
    sides, halves, parts, high, _, _ = spec_ref.shape
    _, per, _, row_count, width = held.shape
    sources = row_count // (halves * SUB)
    first = lax.axis_index("real") * sources
    each = per // 2
    lane = lax.broadcasted_iota(jnp.int32, (2 * row_count, sides * FT), 1)
    band = lane % (FT // 2) // FB

    def gathered(side, j, at, count):
        parts_of = [
            spec_ref[side, h, at, j].astype(jnp.float32).reshape(count, 2, SUB, FT)
            for h in range(halves)
        ]
        return [
            jnp.stack([p[:, i] for p in parts_of], axis=1).reshape(count * halves * SUB, FT)
            for i in range(2)
        ]

    def turned(x):
        moved = pltpu.roll(x, FT // 2, 1)
        at = lax.broadcasted_iota(jnp.int32, x.shape, 1)
        return jnp.where(at < FT // 2, moved, -moved)

    def out_copy(j):
        return pltpu.make_async_copy(held.at[j], out_ref.at[pl.ds(j * per, per)], sems.at[j])

    def one_high(j, carry):
        cols = [gathered(side, j, pl.ds(0, parts), parts) for side in range(sides)]
        own = [gathered(side, j, pl.ds(first, sources), sources) for side in range(sides)]
        for i in range(2):
            col = jnp.concatenate([c[i] for c in cols], axis=1).astype(HALF)
            row = jnp.concatenate(
                [
                    jnp.concatenate([o[i] for o in own], axis=1),
                    jnp.concatenate([turned(o[i]) for o in own], axis=1),
                ],
                axis=0,
            ).astype(HALF)
            for g in range(each):
                kept = jnp.where(band == g, row, jnp.zeros_like(row))
                out = lax.dot_general(
                    kept, col, (((1,), (1,)), ((), ())), preferred_element_type=jnp.float32
                )
                held[j, i * each + g] = (out * scale).reshape(2, row_count, width)
        out_copy(j).start()
        return carry

    lax.fori_loop(0, high, one_high, 0)
    for j in range(high):
        out_copy(j).wait()


def gram(spectra, row_count, scale):
    sides, halves, parts, high, _, _ = spectra.shape
    width = parts * halves * SUB
    per = FT // FB
    shape = (per, 2, row_count, width)
    return pl.pallas_call(
        functools.partial(gram_kernel, scale),
        out_shape=jax.ShapeDtypeStruct((high * per,) + shape[1:], jnp.float32),
        in_specs=[pl.BlockSpec(memory_space=VMEM)],
        out_specs=pl.BlockSpec(memory_space=ANY),
        scratch_shapes=[VMEM((high,) + shape, jnp.float32), pltpu.SemaphoreType.DMA((high,))],
        compiler_params=pltpu.CompilerParams(vmem_limit_bytes=24 * 1024 * 1024),
    )(spectra)


def tiled_shards(input_field, kerr_coeff, block_list):
    parts, sides = lax.axis_size("mode"), lax.axis_size("real")
    _, _, modes, times = input_field.shape
    width = parts * modes
    spectra = spectra_of(
        input_field.reshape(2, modes, times), kerr_coeff[0], block_list, parts, sides
    )
    return gram(spectra, width // sides, 1.0 / (FB * sides))


def tiles_fit(mesh):
    parts = mesh.shape["mode"]
    return FT % parts == 0 and (2 * FT // parts) % 16 == 0 and mesh.shape["real"] <= 2


def either(mesh, input_field, kerr_coeff, block_list):
    modes = input_field.shape[2]
    blocks_each = kerr_coeff.shape[0]
    fits = tiles_fit(mesh) and modes % 16 == 0 and blocks_each == 1
    fits = fits and input_field.shape[1] == 1 and input_field.shape[3] == NT
    return (tiled_shards if fits else shards)(input_field, kerr_coeff, block_list)


def solution(mesh):
    return jax.shard_map(
        functools.partial(either, mesh),
        mesh=mesh,
        in_specs=(P(None, "real", "mode", None), P("mode", None, None), P("mode", None)),
        out_specs=P("mode", None, "real", None),
        check_vma=False,
    )
```

```python
import functools
import math

import jax
import jax.numpy as jnp
import numpy as np
from jax import lax
from jax.experimental import pallas as pl
from jax.experimental.pallas import tpu as pltpu
from jax.sharding import PartitionSpec as P

MB = 8
FT = 128
NT = 16384
FB = 32


kerr_strength = 0.25


def kerr_terms(field_blocks, coeff_group, block_group):
    mode_l = jnp.take(field_blocks, block_group[:, 1], axis=2).astype(jnp.float32)
    mode_m = jnp.take(field_blocks, block_group[:, 2], axis=2).astype(jnp.float32)
    mode_n = jnp.take(field_blocks, block_group[:, 3], axis=2).astype(jnp.float32)
    realiz = field_blocks.shape[1]
    group_size = block_group.shape[0]
    steps_local = field_blocks.shape[4]
    prod_re = (
        mode_m[0][:, :, :, None, :] * mode_n[0][:, :, None, :, :]
        + mode_m[1][:, :, :, None, :] * mode_n[1][:, :, None, :, :]
    )
    prod_im = (
        mode_m[1][:, :, :, None, :] * mode_n[0][:, :, None, :, :]
        - mode_m[0][:, :, :, None, :] * mode_n[1][:, :, None, :, :]
    )
    pairs = (
        jnp.stack([prod_re, prod_im])
        .reshape(2, realiz, group_size, MB * MB, steps_local)
        .astype(jnp.bfloat16)
    )
    weighted = jnp.einsum(
        "kab,crkbt->crkat", coeff_group, pairs, preferred_element_type=jnp.float32
    )
    weighted = weighted.reshape(2, realiz, group_size, MB, MB, steps_local)
    term_re = jnp.sum(
        weighted[0] * mode_l[0][:, :, None] - weighted[1] * mode_l[1][:, :, None], axis=3
    )
    term_im = jnp.sum(
        weighted[0] * mode_l[1][:, :, None] + weighted[1] * mode_l[0][:, :, None], axis=3
    )
    one_hot = (
        block_group[:, 0][:, None] == jnp.arange(field_blocks.shape[2], dtype=jnp.int32)[None, :]
    ).astype(jnp.float32)
    return jnp.einsum(
        "kg,crkpt->crgpt", one_hot, jnp.stack([term_re, term_im]), precision=lax.Precision.HIGHEST
    )


def phase_table(extent, modulus):
    index_a = jnp.arange(extent, dtype=jnp.int32)[:, None]
    index_b = jnp.arange(extent, dtype=jnp.int32)[None, :]
    angle = 2.0 * math.pi / modulus * (index_a * index_b % modulus).astype(jnp.float32)
    return (jnp.cos(angle), -jnp.sin(angle))


def first_pass(table, data):
    table_high = table.astype(jnp.bfloat16)
    table_low = (table - table_high.astype(jnp.float32)).astype(jnp.bfloat16)
    upper = jnp.einsum("kn,rmnj->rmkj", table_high, data, preferred_element_type=jnp.float32)
    return upper + jnp.einsum("kn,rmnj->rmkj", table_low, data, preferred_element_type=jnp.float32)


def second_pass(table, data):
    return jnp.einsum("jn,rmkn->rmjk", table, data, precision=lax.Precision.HIGH)


def transform(by_mode):
    realiz = by_mode.shape[1]
    local_modes = by_mode.shape[2]
    signal = by_mode.reshape(2, realiz, local_modes, FT, FT)
    four_re, four_im = phase_table(FT, FT)
    twist_re, twist_im = phase_table(FT, NT)
    half_re = first_pass(four_re, signal[0]) - first_pass(four_im, signal[1])
    half_im = first_pass(four_re, signal[1]) + first_pass(four_im, signal[0])
    turned_re = half_re * twist_re - half_im * twist_im
    turned_im = half_re * twist_im + half_im * twist_re
    out_re = (second_pass(four_re, turned_re) - second_pass(four_im, turned_im)) / FT
    out_im = (second_pass(four_re, turned_im) + second_pass(four_im, turned_re)) / FT
    return jnp.stack([out_re, out_im]).astype(jnp.bfloat16)


def gram_parts(rows_part, cols_part):
    mode_parts = jnp.einsum(
        "crpbf,drqbf->bcdpq", rows_part, cols_part, preferred_element_type=jnp.float32
    )
    return jnp.stack(
        [mode_parts[:, 0, 0] + mode_parts[:, 1, 1], mode_parts[:, 1, 0] - mode_parts[:, 0, 1]], axis=1
    )


def shards(input_field, kerr_coeff, block_list):
    timed = lax.all_to_all(input_field, "mode", split_axis=3, concat_axis=2, tiled=True)
    realiz = timed.shape[1]
    width = timed.shape[2]
    steps_local = timed.shape[3]
    field_blocks = timed.reshape(2, realiz, width // MB, MB, steps_local)
    initial = jnp.zeros(field_blocks.shape, jnp.float32)
    running = initial
    coeff_piece = lax.all_gather(kerr_coeff, "mode", axis=0, tiled=True)
    block_piece = lax.all_gather(block_list, "mode", axis=0, tiled=True)
    block_count = block_piece.shape[0]
    coeff_groups = coeff_piece.reshape(
        block_count // 8, 8, coeff_piece.shape[1], coeff_piece.shape[2]
    )
    block_groups = block_piece.reshape(block_count // 8, 8, 4)

    def one_group(carried, groups):
        return (carried + kerr_terms(field_blocks, groups[0], groups[1]), None)

    running, unused = lax.scan(one_group, running, (coeff_groups, block_groups))
    kerr_sum = running
    kerr_sum = kerr_sum.reshape(2, realiz, width, steps_local)
    base = timed.astype(jnp.float32)
    stepped = jnp.stack(
        [base[0] - kerr_strength * kerr_sum[1], base[1] + kerr_strength * kerr_sum[0]]
    ).astype(jnp.bfloat16)
    by_mode = lax.all_to_all(stepped, "mode", split_axis=2, concat_axis=3, tiled=True)
    spectrum = transform(by_mode)
    banded = lax.all_to_all(spectrum, "mode", split_axis=3, concat_axis=2, tiled=True)
    bands_dev = banded.shape[3] * FT // FB
    spec_bands = banded.reshape(2, realiz, width, bands_dev, FB)
    scale = 1.0 / (FB * realiz * lax.axis_size("real"))
    row_count = width // lax.axis_size("real")
    row_first = lax.axis_index("real") * row_count
    shard_piece = lax.all_gather(spec_bands, "real", axis=1, tiled=True)
    own_part = lax.dynamic_slice_in_dim(shard_piece, row_first, row_count, 2)
    return gram_parts(own_part, shard_piece) * scale


VMEM = pltpu.VMEM
ANY = pl.ANY
HALF = jnp.bfloat16
SUB = 8


def plane_size(parts):
    return 4 if parts % 4 == 0 else 1


def partner_order(parts):
    return list(range(1, parts))


def partner(me, step):
    to, bit = me, 1
    while bit <= step:
        if step & bit:
            to = to + bit - 2 * bit * (me // bit % 2)
        bit *= 2
    return to


def remote(here, there, sent, landed, target):
    copy = pltpu.make_async_remote_copy(
        src_ref=here,
        dst_ref=there,
        send_sem=sent,
        recv_sem=landed,
        device_id=target,
        device_id_type=pl.DeviceIdType.MESH,
    )
    copy.start()
    return copy


def local(here, there, sem):
    copy = pltpu.make_async_copy(here, there, sem)
    copy.start()
    return copy


def kerr_terms_of(k, at, piece, list_s, coef, fld, terms):
    span = pl.ds(0, piece)
    bl, bm, bn = (list_s[*at, 0, i] for i in (1, 2, 3))
    m_re, m_im = fld[0, bm, :, span][:, None], fld[1, bm, :, span][:, None]
    n_re, n_im = fld[0, bn, :, span][None], fld[1, bn, :, span][None]
    p_re = (m_re * n_re + m_im * n_im).reshape(MB * MB, piece)
    p_im = (m_im * n_re - m_re * n_im).reshape(MB * MB, piece)
    pairs = jnp.concatenate([p_re, p_im], axis=1).astype(HALF)
    w = jnp.dot(coef, pairs, preferred_element_type=jnp.float32)
    w_re = w[:, :piece].reshape(MB, MB, piece)
    w_im = w[:, piece:].reshape(MB, MB, piece)
    l_re, l_im = fld[0, bl, :, span][:, None], fld[1, bl, :, span][:, None]
    row = pl.ds(pl.multiple_of(k * MB, MB), MB)
    terms[0, row, span] = jnp.sum(w_re * l_re - w_im * l_im, axis=0)
    terms[1, row, span] = jnp.sum(w_re * l_im + w_im * l_re, axis=0)


def owner_table(blocks, width, list_s):
    shape = (width, blocks * MB)
    row = lax.broadcasted_iota(jnp.int32, shape, 0)
    col = lax.broadcasted_iota(jnp.int32, shape, 1)
    wanted = jnp.full(shape, -1, jnp.int32)
    plane = plane_size(blocks)
    for k in range(blocks):
        wanted = jnp.where(col // MB == k, list_s[k % plane, k // plane, 0, 0] * MB + col % MB, wanted)
    return (row == wanted).astype(jnp.float32).astype(HALF)


def swap_rows(coef):
    order_of = (MB * MB, MB * MB)
    row = lax.broadcasted_iota(jnp.int32, order_of, 0)
    col = lax.broadcasted_iota(jnp.int32, order_of, 1)
    swap = (col == (row % MB) * MB + row // MB).astype(jnp.float32).astype(HALF)
    return jnp.dot(swap, coef, preferred_element_type=jnp.float32).astype(HALF)


def pack_coef(coef):
    rows = coef.shape[0] // 2
    return jnp.concatenate([coef[:rows], coef[rows:]], axis=1)


def unpack_coef(pieces):
    packed = jnp.concatenate(pieces, axis=0)
    lanes = packed.shape[1] // 2
    return jnp.concatenate([packed[:, :lanes], packed[:, lanes:]], axis=0)


def whole_kernel(parts, sides, cuts, x_ref, coef_ref, list_ref, *refs):
    table_refs, out_ref = refs[:6], refs[6]
    (timed, coef_in, coef_own, coefs, lists, list_s, fld, terms, stepped, by_mode, xf, rows, spec) = refs[7:20]
    tables, (sends, recvs, own_sems) = refs[20:26], refs[26:]
    me = lax.axis_index("mode")
    other = {"real": 1 - lax.axis_index("real")}
    _, modes, times = x_ref.shape
    steps = times // parts
    width = parts * modes
    groups = width // MB
    fine = steps // FT
    pieces = len(cuts)
    starts = [sum(cuts[:part]) for part in range(pieces)]
    halves = modes // SUB
    order = partner_order(parts)
    plane = plane_size(parts)
    barrier = pltpu.get_barrier_semaphore()
    for step in reversed(order):
        to = {"mode": partner(me, step)}
        pl.semaphore_signal(barrier, inc=1, device_id=to, device_id_type=pl.DeviceIdType.MESH)
    if sides > 1:
        pl.semaphore_signal(barrier, inc=1, device_id=other, device_id_type=pl.DeviceIdType.MESH)

    local(coef_ref, coef_in, own_sems.at[0]).wait()
    early = [local(a, b, own_sems.at[4 + i]) for i, (a, b) in enumerate(zip(table_refs, tables))]
    coef_own[...] = pack_coef(swap_rows(coef_in[...])).reshape(coef_own.shape)
    pl.semaphore_wait(barrier, parts - 1 + (sides > 1))

    slot = iter(range(sends.shape[0]))
    column, row_of = me % plane, me // plane

    def columns_ascending():
        pairs = []
        for i in range(plane - 1):
            to = i + (i - column + plane) // plane
            step, bit = 0, 1
            while bit < plane:
                step = step + (to // bit + column // bit) % 2 * bit
                bit *= 2
            pairs.append((row_of * plane + to, step))
        for r in range(1, parts // plane):
            for k in range(plane):
                row = partner(me, r * plane) // plane
                pairs.append((row * plane + k, r * plane + partner(column, k)))
        return pairs

    targets = columns_ascending()

    def send_to_all(here, there):
        at = next(slot)
        return [
            remote(here(to), there, sends.at[at, step], recvs.at[at, step], {"mode": to})
            for to, step in targets
        ]

    def send_all(here, there, steps_of=order):
        at = next(slot)
        return [
            remote(here(partner(me, step)), there, sends.at[at, step], recvs.at[at, step],
                   {"mode": partner(me, step)})
            for step in steps_of
        ]

    side = lax.axis_index("real")
    own_coef = coefs.at[side, column, row_of]
    mine = coef_own.at[side]
    first = send_all(lambda to: mine, own_coef, [step for step in order if step % plane == 0])
    first.append(local(mine, own_coef, own_sems.at[0]))
    own_list = lists.at[column, row_of]
    first += send_all(lambda to: list_ref, own_list, [step for step in order if step % plane == 0])
    first.append(local(list_ref, own_list, own_sems.at[1]))

    def chunk(to, part):
        at = pl.multiple_of(to * steps + starts[part] * FT, FT)
        return x_ref.at[:, :, pl.ds(at, cuts[part] * FT)]

    def landing(part):
        return timed.at[me, :, :, pl.ds(starts[part] * FT, cuts[part] * FT)]

    def send_field(part):
        copies = send_all(lambda to: chunk(to, part), landing(part))
        copies.append(local(chunk(me, part), landing(part), own_sems.at[10 + part]))
        return copies

    field_copies = [send_field(0)]
    for copy in first:
        copy.wait()
    near = [step for step in order if step < plane]
    listed = send_all(lambda to: lists.at[column], lists.at[column], near)
    second = send_all(lambda to: coefs.at[side, column], coefs.at[side, column], near)
    field_copies += [send_field(part) for part in range(1, pieces)]
    for copy in listed:
        copy.wait()
    local(lists, list_s, own_sems.at[2]).wait()
    owners = owner_table(parts, width, list_s)
    for copy in second:
        copy.wait()
    if sides > 1:
        at = next(slot)
        remote(coefs.at[side], coefs.at[side], sends.at[at, 0], recvs.at[at, 0], other).wait()

    mode_copies = [[] for _ in range(halves)]

    def send_stepped(h, first_tile, tiles):
        some = pl.ds(first_tile // 2, tiles // 2)
        copies = send_to_all(lambda to: stepped.at[h, to, some], by_mode.at[h, me, some])
        at = own_sems.at[20 + halves * pieces + h if tiles == fine else 20 + h * pieces + starts.index(first_tile)]
        copies.append(local(stepped.at[h, me, some], by_mode.at[h, me, some], at))
        mode_copies[h].append((first_tile, tiles, copies))

    for part, copies in enumerate(field_copies):
        for copy in copies:
            copy.wait()
        tiles = cuts[part]
        half = tiles * FT
        here, span = pl.ds(0, half), pl.ds(starts[part] * FT, half)
        for c in range(2):
            fld[c, :, :, here] = timed[:, c, :, span].astype(jnp.float32).reshape(groups, MB, half)

        def one_block(k, carry):
            at = (k % plane, k // plane)
            coef = unpack_coef([coefs[i, *at] for i in range(sides)])
            kerr_terms_of(k, at, half, list_s, coef, fld, terms)
            return carry

        lax.fori_loop(0, parts, one_block, 0, unroll=2)
        for c in range(2):
            term = terms[1 - c, :, here]
            high = term.astype(HALF)
            low = (term - high.astype(jnp.float32)).astype(HALF)
            kerr = jnp.dot(owners, high, preferred_element_type=jnp.float32)
            kerr = kerr + jnp.dot(owners, low, preferred_element_type=jnp.float32)
            turn = kerr_strength * (2 * c - 1)
            new = fld[c, :, :, here].reshape(width, half) + turn * kerr
            new = new.reshape(parts, halves, SUB, half)
            for h in range(halves):
                for n in range(0, tiles, 2):
                    pair = [new[:, h, :, (n + i) * FT : (n + i + 1) * FT] for i in range(2)]
                    stepped[h, :, (starts[part] + n) // 2, c] = jnp.concatenate(pair, axis=1).astype(HALF)
        send_stepped(0, starts[part], tiles)
    for h in range(1, halves):
        send_stepped(h, 0, fine)
    for copy in early:
        copy.wait()

    def send_spectra(h):
        at = next(slot)
        copies = [
            remote(spec.at[h, to], out_ref.at[0, h, me], sends.at[at, step], recvs.at[at, step], {"mode": to})
            for to, step in targets
        ]
        own = local(spec.at[h, me], out_ref.at[0, h, me], own_sems.at[3 if h else 0])
        return copies, own, at

    def arrived(h, at, step):
        source = partner(me, step)
        pltpu.make_async_remote_copy(
            src_ref=spec.at[h, source],
            dst_ref=out_ref.at[0, h, source],
            send_sem=sends.at[at, step],
            recv_sem=recvs.at[at, step],
            device_id={"mode": source},
            device_id_type=pl.DeviceIdType.MESH,
        ).wait_recv()

    def passing(h, some, at, which):
        if sides == 1:
            return []
        here, there = out_ref.at[0, h, some], out_ref.at[1, h, some]
        return [remote(here, there, sends.at[at, which], recvs.at[at, which], other)]

    outgoing = []
    for h in range(halves):
        for first_tile, tiles, copies in mode_copies[h]:
            for copy in copies:
                copy.wait()
            for n in range(first_tile, first_tile + tiles, 2):
                for c in range(2):
                    pair = by_mode[h, :, n // 2, c].astype(jnp.float32)
                    xf[c, :, n : n + 2] = pair.reshape(parts, 2, SUB, FT)
        dft_modes(xf, rows, tables)
        spec[h] = pair_lanes(rows[...]).reshape(spec.shape[1:]).astype(HALF)
        outgoing.append(send_spectra(h))
    passed = []
    for h, (copies, own, at) in enumerate(outgoing):
        pass_at = next(slot)
        own.wait()
        for r in range(parts // plane):
            row = partner(me, r * plane) // plane
            for step in range(r * plane, (r + 1) * plane):
                if step:
                    arrived(h, at, step)
            if h == halves - 1:
                passed += passing(h, pl.ds(row * plane, plane), pass_at, r)
        if h < halves - 1:
            passed += passing(h, pl.ds(0, parts), pass_at, 0)
    for copies, _, _ in outgoing:
        for copy in copies:
            copy.wait_send()
    for copy in passed:
        copy.wait()


def spectra_of(field, coef, listed, parts, sides):
    _, modes, times = field.shape
    steps = times // parts
    width = parts * modes
    fine = steps // FT
    halves = modes // SUB
    cuts = [fine // 2, fine // 2]
    pieces = len(cuts)
    half = max(cuts) * FT
    plane = plane_size(parts)
    tables = dft_tables()
    slots = 5 + pieces * 2 + 3 * halves
    packed = (coef.shape[0] // 2 // sides, coef.shape[1] * 2)
    spread = (halves, parts, fine, 2 * SUB, FT)
    return pl.pallas_call(
        functools.partial(whole_kernel, parts, sides, cuts),
        out_shape=jax.ShapeDtypeStruct((sides,) + spread, HALF),
        in_specs=[pl.BlockSpec(memory_space=pltpu.HBM)] * (3 + len(tables)),
        out_specs=pl.BlockSpec(memory_space=ANY),
        scratch_shapes=[
            VMEM((parts, 2, modes, steps), HALF),
            VMEM(coef.shape, HALF),
            VMEM((sides,) + packed, HALF),
            VMEM((sides, plane, parts // plane) + packed, HALF),
            VMEM((plane, parts // plane) + listed.shape, jnp.int32),
            pltpu.SMEM((plane, parts // plane) + listed.shape, jnp.int32),
            VMEM((2, width // MB, MB, half), jnp.float32),
            VMEM((2, parts * MB, half), jnp.float32),
            VMEM((halves, parts, fine // 2, 2, 2 * SUB, FT), HALF),
            VMEM((halves, parts, fine // 2, 2, 2 * SUB, FT), HALF),
            VMEM((2, parts, fine, SUB, FT), jnp.float32),
            VMEM((2 * FT * SUB, FT), jnp.float32),
            VMEM(spread, HALF),
        ]
        + [VMEM(t.shape, t.dtype) for t in tables]
        + [
            pltpu.SemaphoreType.DMA((slots, parts)),
            pltpu.SemaphoreType.DMA((slots, parts)),
            pltpu.SemaphoreType.DMA((20 + (pieces + 1) * halves,)),
        ],
        compiler_params=pltpu.CompilerParams(
            collective_id=0, has_side_effects=True, vmem_limit_bytes=28 * 1024 * 1024
        ),
    )(*(pltpu.with_memory_space_constraint(a, pltpu.HBM) for a in (field, coef, listed, *tables)))


def dft_tables():
    a = np.arange(FT)
    four = np.exp(-2j * np.pi / FT * (np.outer(a, a) % FT))
    twist = np.exp(-2j * np.pi / NT * (np.outer(a, a) % NT)) / FT
    first = np.block([[four.real, -four.imag], [four.imag, four.real]])
    second = first.reshape(2, FT, 2 * FT).transpose(1, 0, 2).reshape(2 * FT, 2 * FT)

    def split(t):
        t = t.astype(np.float32)
        high = t.astype(HALF)
        return high, (t - high.astype(np.float32)).astype(HALF)

    return (
        *split(first),
        twist.real.astype(np.float32),
        twist.imag.astype(np.float32),
        *split(second),
    )


def dft_modes(xf, rows, tables):
    f1h, f1l, tw_re, tw_im, f2h, f2l = tables
    flat = xf.reshape(2 * FT * SUB, FT)
    nt = (((1,), (1,)), ((), ()))
    dot = functools.partial(jnp.dot, preferred_element_type=jnp.float32)
    dot_nt = functools.partial(
        lax.dot_general, dimension_numbers=nt, preferred_element_type=jnp.float32
    )
    for m in range(0, SUB, 2):
        x = jnp.concatenate(
            [flat[pl.ds(m + i, 2 * FT, stride=SUB), :].astype(HALF) for i in range(2)], axis=1
        )
        half = dot(f1h[...], x) + dot(f1l[...], x)
        turned = []
        for i in range(2):
            h_re, h_im = half[:FT, i * FT : (i + 1) * FT], half[FT:, i * FT : (i + 1) * FT]
            turned.append(
                jnp.concatenate(
                    [
                        h_re * tw_re[...] - h_im * tw_im[...],
                        h_re * tw_im[...] + h_im * tw_re[...],
                    ],
                    axis=1,
                )
            )
        turned = jnp.concatenate(turned, axis=0)
        high = turned.astype(HALF)
        low = (turned - high.astype(jnp.float32)).astype(HALF)
        out = dot_nt(f2h[...], high) + dot_nt(f2h[...], low) + dot_nt(f2l[...], high)
        for i in range(2):
            rows[pl.ds(m + i, 2 * FT, stride=SUB), :] = out[:, i * FT : (i + 1) * FT]


def pair_lanes(rows):
    both = rows.reshape(FT, 2, SUB, FT)
    re, im = both[:, 0], both[:, 1]
    left = lax.broadcasted_iota(jnp.int32, re.shape, 2) < FT // 2
    low = jnp.where(left, re, pltpu.roll(im, FT // 2, 2))
    high = jnp.where(left, pltpu.roll(re, FT // 2, 2), im)
    return jnp.stack([low, high], axis=1)


def gram_kernel(scale, spec_ref, out_ref, held, sems):
    sides, halves, parts, high, _, _ = spec_ref.shape
    _, per, _, row_count, width = held.shape
    sources = row_count // (halves * SUB)
    first = lax.axis_index("real") * sources
    each = per // 2
    lane = lax.broadcasted_iota(jnp.int32, (2 * row_count, sides * FT), 1)
    band = lane % (FT // 2) // FB

    def gathered(side, j, at, count):
        parts_of = [
            spec_ref[side, h, at, j].astype(jnp.float32).reshape(count, 2, SUB, FT)
            for h in range(halves)
        ]
        return [
            jnp.stack([p[:, i] for p in parts_of], axis=1).reshape(count * halves * SUB, FT)
            for i in range(2)
        ]

    def turned(x):
        moved = pltpu.roll(x, FT // 2, 1)
        at = lax.broadcasted_iota(jnp.int32, x.shape, 1)
        return jnp.where(at < FT // 2, moved, -moved)

    def out_copy(j):
        return pltpu.make_async_copy(held.at[j], out_ref.at[pl.ds(j * per, per)], sems.at[j])

    def one_high(j, carry):
        cols = [gathered(side, j, pl.ds(0, parts), parts) for side in range(sides)]
        own = [gathered(side, j, pl.ds(first, sources), sources) for side in range(sides)]
        for i in range(2):
            col = jnp.concatenate([c[i] for c in cols], axis=1).astype(HALF)
            row = jnp.concatenate(
                [
                    jnp.concatenate([o[i] for o in own], axis=1),
                    jnp.concatenate([turned(o[i]) for o in own], axis=1),
                ],
                axis=0,
            ).astype(HALF)
            for g in range(each):
                kept = jnp.where(band == g, row, jnp.zeros_like(row))
                out = lax.dot_general(
                    kept, col, (((1,), (1,)), ((), ())), preferred_element_type=jnp.float32
                )
                held[j, i * each + g] = (out * scale).reshape(2, row_count, width)
        out_copy(j).start()
        return carry

    lax.fori_loop(0, high, one_high, 0)
    for j in range(high):
        out_copy(j).wait()


def gram(spectra, row_count, scale):
    sides, halves, parts, high, _, _ = spectra.shape
    width = parts * halves * SUB
    per = FT // FB
    shape = (per, 2, row_count, width)
    return pl.pallas_call(
        functools.partial(gram_kernel, scale),
        out_shape=jax.ShapeDtypeStruct((high * per,) + shape[1:], jnp.float32),
        in_specs=[pl.BlockSpec(memory_space=VMEM)],
        out_specs=pl.BlockSpec(memory_space=ANY),
        scratch_shapes=[VMEM((high,) + shape, jnp.float32), pltpu.SemaphoreType.DMA((high,))],
        compiler_params=pltpu.CompilerParams(vmem_limit_bytes=24 * 1024 * 1024),
    )(spectra)


def tiled_shards(input_field, kerr_coeff, block_list):
    parts, sides = lax.axis_size("mode"), lax.axis_size("real")
    _, _, modes, times = input_field.shape
    width = parts * modes
    spectra = spectra_of(
        input_field.reshape(2, modes, times), kerr_coeff[0], block_list, parts, sides
    )
    return gram(spectra, width // sides, 1.0 / (FB * sides))


def tiles_fit(mesh):
    parts = mesh.shape["mode"]
    return FT % parts == 0 and (2 * FT // parts) % 16 == 0 and mesh.shape["real"] <= 2


def either(mesh, input_field, kerr_coeff, block_list):
    modes = input_field.shape[2]
    blocks_each = kerr_coeff.shape[0]
    fits = tiles_fit(mesh) and modes % 16 == 0 and blocks_each == 1
    fits = fits and input_field.shape[1] == 1 and input_field.shape[3] == NT
    return (tiled_shards if fits else shards)(input_field, kerr_coeff, block_list)


def solution(mesh):
    return jax.shard_map(
        functools.partial(either, mesh),
        mesh=mesh,
        in_specs=(P(None, "real", "mode", None), P("mode", None, None), P("mode", None)),
        out_specs=P("mode", None, "real", None),
        check_vma=False,
    )
```
